32 devices in a mesh: seq: 16 (over z, x, core), head: 2 (over y).
Axes of the slice: x: 2, y: 2, z: 4, core: 2. Of those that a mesh axis runs over, the one named last changes fastest.
Arguments:
- queries: bfloat16 [4096, 4096], P(('seq', 'head')), may hold values from -130 to 130
- keys: bfloat16 [4096, 1024], P(('seq', 'head')), may hold values from -5 to 5
- values: bfloat16 [4096, 1024], P(('seq', 'head')), may hold values from -6 to 6
- vertical: int32 [8, 128], P('head'), may hold values from 0 to 4095, as said below
- slash: int32 [8, 64, 40], P('head'), may hold values from -1 to 59, as said below
Outputs:
- attended: bfloat16 [4096, 4096], P(('seq', 'head'))
The draws below stay inside these ranges and needn't reach their ends.
Inputs may be any that keep to these rules, and one draw needn't show every extreme that they name: `vertical`: for each KV head the 128 entries are distinct token positions; the 256 tokens of one seq shard hold at most 15 of them, and for every head some seq shard holds exactly that many. Each KV head h has 40 distinct block offsets d[h, n], each at least 4, and some offset of every head equals 4; slash[h, b, n] = b - d[h, n] where that is not negative, else -1.
All inputs are finite; a program needn't handle non-finite values.
Results may differ from the reference program's by a relative error of at most 0.0052.
Values may be sent and summed in bfloat16 or wider, within the bound.
No kernel may reach another device: no remote copies, remote signals or barrier semaphores. Data moves between devices by JAX's collectives and lax.ppermute only.
A program may use at most 128 MiB of HBM per device.

```python
import math
import jax
import jax.numpy as jnp
from jax import lax

Q_HEADS = 32
KV_HEADS = 8
HD = 128
BLK = 64
NS = 40
VERT_DEV = 8
TOK_DEV = 256
TOKENS = 4096
QBLOCKS = 64
NV = 128


def paired_fields(key):
    key_keys = jax.random.fold_in(key, 11)
    key_query = jax.random.fold_in(key, 12)
    key_field = jnp.clip(jax.random.normal(key_keys, (TOKENS, KV_HEADS, HD), jnp.float32), -5.0, 5.0)
    query_field = jnp.clip(1.5 * jax.random.normal(key_query, (TOKENS, Q_HEADS, HD), jnp.float32), -7.5, 7.5)
    return (query_field, key_field)


def draw_queries(key, part):
    query_field, key_field = paired_fields(key)
    return query_field.reshape(TOKENS, Q_HEADS * HD).astype(jnp.bfloat16)


def draw_keys(key, part):
    query_field, key_field = paired_fields(key)
    return key_field.reshape(TOKENS, KV_HEADS * HD).astype(jnp.bfloat16)


def draw_vertical(key, part):
    shards = TOKENS // TOK_DEV
    half = shards // 2
    room = 2 * VERT_DEV - 1

    def offsets_of(shard_key):
        return jax.random.permutation(shard_key, TOK_DEV)[:room]

    def one_head(head_key):
        key_order, key_delta, key_place = jax.random.split(head_key, 3)
        order = jax.random.permutation(key_order, shards)
        delta = jax.random.randint(key_delta, (half,), 0, VERT_DEV)
        delta = delta.at[0].set(VERT_DEV - 1)
        signed = jnp.concatenate([delta, -delta])
        counts = jnp.zeros((shards,), jnp.int32).at[order].set(VERT_DEV + signed)
        offsets = jax.vmap(offsets_of)(jax.random.split(key_place, shards))
        slots = jnp.arange(room)
        valid = slots[None, :] < counts[:, None]
        index = offsets + jnp.arange(shards)[:, None] * TOK_DEV
        flat_valid = valid.reshape(-1)
        flat_index = index.reshape(-1)
        length = flat_index.shape[0]
        priority = jnp.where(flat_valid, 0, 1) * length + jnp.arange(length)
        picked = jnp.argsort(priority)[:NV]
        return flat_index[picked].astype(jnp.int32)
    return jax.vmap(one_head)(jax.random.split(key, KV_HEADS)).astype(jnp.int32)


def draw_slash(key, part):
    per_block = TOK_DEV // BLK
    span = QBLOCKS - per_block

    def one_head(head_key):
        key_pick, key_order = jax.random.split(head_key, 2)
        rest = jax.random.permutation(key_pick, span - 1)[:NS - 1] + 1
        offsets = jnp.concatenate([jnp.zeros((1,), jnp.int32), rest.astype(jnp.int32)]) + per_block
        offsets = jax.random.permutation(key_order, offsets)
        block = jnp.arange(QBLOCKS, dtype=jnp.int32)[:, None]
        entry = block - offsets[None, :]
        return jnp.where(entry >= 0, entry, -1).astype(jnp.int32)
    return jax.vmap(one_head)(jax.random.split(key, KV_HEADS)).astype(jnp.int32)


def level_of(stream_key, shape, cuts, smallest, high):
    def one(position, blocks):
        draws = jax.random.uniform(jax.random.fold_in(jax.random.fold_in(stream_key, 6), position), (blocks,), jnp.float32, smallest / len(cuts), high / len(cuts))
        return jnp.repeat(jnp.exp(draws), shape[position] // blocks).reshape((-1,) + (1,) * (len(shape) - position - 1))

    level = one(*cuts[0])
    for cut in cuts[1:]:
        level = level * one(*cut)
    return level


def gaussian(own_key, extent, deviation, limit, cuts=(), held_as=jnp.bfloat16):
    drawn = deviation * jax.random.normal(own_key, extent, jnp.float32)
    if cuts:
        drawn = drawn * level_of(own_key, extent, cuts, -0.22, 0.18)
    return jnp.clip(drawn, -limit, limit).astype(held_as)


def setup_inputs(seed: int = 0) -> dict:
    seeds = jax.random.split(jax.random.key(seed), 6)
    return {
        "queries": draw_queries(jax.random.fold_in(seeds[5], 71), 0),
        "keys": draw_keys(jax.random.fold_in(seeds[5], 71), 0),
        "values": gaussian(seeds[2], (TOKENS, KV_HEADS * HD), 1.0, 6.0, ((0, 32),)),
        "vertical": draw_vertical(jax.random.fold_in(seeds[5], 71), 0),
        "slash": draw_slash(jax.random.fold_in(seeds[5], 71), 0),
    }


def live_entries(lists):
    count = lists.shape[-1]
    earlier = jnp.arange(count)[:, None] > jnp.arange(count)[None, :]
    repeated = jnp.any(earlier & (lists[..., :, None] == lists[..., None, :]), axis=-1)
    return (lists >= 0) & jnp.logical_not(repeated)

def block_attention(query_part, diag_part, slash_part, slash_live, slash_list, vert_part, vert_where, block_ids, head_dim, operand_type):
    scaling = 1.0 / math.sqrt(head_dim)
    width = query_part.shape[1]
    steps = query_part.shape[0]
    rows = query_part.shape[2]
    listed = slash_part.shape[1]
    positions = block_ids[:, None] * width + jnp.arange(width, dtype=jnp.int32)[None, :]
    first = jnp.einsum('gqrd,gkd->gqrk', query_part, diag_part[..., :head_dim], preferred_element_type=jnp.float32) * scaling
    causal = jnp.arange(width)[None, :] <= jnp.arange(width)[:, None]
    first = jnp.where(causal[None, :, None, :], first, -jnp.inf)
    second = jnp.einsum('gqrd,gnkd->gqrnk', query_part, slash_part[..., :head_dim], preferred_element_type=jnp.float32) * scaling
    second = jnp.where(slash_live[:, None, None, :, None], second, -jnp.inf)
    second = second.reshape(steps, width, rows, listed * width)
    third = jnp.einsum('gqrd,vd->gqrv', query_part, vert_part[:, :head_dim], preferred_element_type=jnp.float32) * scaling
    vert_block = vert_where // width
    covered = (vert_block[None, :] == block_ids[:, None]) | jnp.any(slash_live[:, :, None] & (slash_list[:, :, None] == vert_block[None, None, :]), axis=1)
    visible = (vert_where[None, None, :] <= positions[:, :, None]) & jnp.logical_not(covered)[:, None, :]
    third = jnp.where(visible[:, :, None, :], third, -jnp.inf)
    scores = jnp.concatenate([first, second, third], axis=-1)
    top = lax.optimization_barrier(jnp.max(scores, axis=-1, keepdims=True))
    expo = jnp.exp(scores - top)
    total = lax.optimization_barrier(jnp.sum(expo, axis=-1, keepdims=True))
    weights = (expo / total).astype(jnp.bfloat16).astype(operand_type)
    w_diag = weights[..., :width]
    w_slash = weights[..., width:width + listed * width].reshape(steps, width, rows, listed, width)
    w_vert = weights[..., width + listed * width:]
    out_diag = jnp.einsum('gqrk,gkd->gqrd', w_diag, diag_part[..., head_dim:], preferred_element_type=jnp.float32)
    out_slash = jnp.einsum('gqrnk,gnkd->gqrd', w_slash, slash_part[..., head_dim:], preferred_element_type=jnp.float32)
    out_vert = jnp.einsum('gqrv,vd->gqrd', w_vert, vert_part[:, head_dim:], preferred_element_type=jnp.float32)
    return (out_diag + out_slash + out_vert).astype(jnp.bfloat16)

def reference(queries, keys, values, vertical, slash):
    tokens = keys.shape[0]
    group = Q_HEADS // KV_HEADS
    blocks = tokens // BLK
    steps_count = blocks // 4
    query_all = queries.reshape(steps_count, 4, BLK, KV_HEADS, group, HD)
    paired_all = jnp.concatenate([keys.reshape(tokens, KV_HEADS, HD), values.reshape(tokens, KV_HEADS, HD)], axis=2)

    def per_head(head_index):
        paired = jnp.take(paired_all, head_index, axis=1).astype(jnp.float32)
        paired_blocks = paired.reshape(blocks, BLK, 2 * HD)
        vert_where = jnp.take(vertical, head_index, axis=0).astype(jnp.int32)
        vert_part = paired[vert_where]
        lists = jnp.take(slash, head_index, axis=0).astype(jnp.int32).reshape(steps_count, 4, NS)
        live = live_entries(lists)
        query_head = jnp.take(query_all, head_index, axis=3).astype(jnp.float32)
        diag_all = paired_blocks.reshape(steps_count, 4, BLK, 2 * HD)
        block_ids = jnp.arange(blocks, dtype=jnp.int32).reshape(steps_count, 4)

        def per_step(items):
            query_part, diag_part, slash_list, slash_live, ident = items
            slash_part = paired_blocks[jnp.maximum(slash_list, 0)]
            return block_attention(query_part, diag_part, slash_part, slash_live, slash_list, vert_part, vert_where, ident, HD, jnp.float32)
        return lax.map(per_step, (query_head, diag_all, lists, live, block_ids))
    result = lax.map(per_head, jnp.arange(KV_HEADS, dtype=jnp.int32))
    result = jnp.transpose(result, (1, 2, 3, 0, 4, 5)).reshape(tokens, Q_HEADS * HD)
    return result
```

```python
import functools
import math

import jax
import jax.numpy as jnp
from jax import lax
from jax.experimental import pallas as pl
from jax.experimental.pallas import tpu as pltpu
from jax.sharding import Mesh, PartitionSpec as P

BLK = 64
BIG = 1.0e30
CHUNK = 4


def attention_kernel(
    idx_ref, dead_ref, own_ref, q_ref, vrow_ref, ev_ref, *rest, parts, listed, head_dim, group
):
    kv_parts = rest[:parts]
    out_ref, kv, vt, kvert, vtvert, qext, etile, scores, sems = rest[parts:]
    rows = BLK * group
    part_rows = kv_parts[0].shape[0]
    total = parts * part_rows
    blocks_here = q_ref.shape[0] // BLK
    verts = vrow_ref.shape[0]
    scale = math.log2(math.e) / math.sqrt(head_dim)
    copies = [
        pltpu.make_async_copy(part, kv.at[pl.ds(i * part_rows, part_rows), :], sems.at[i])
        for i, part in enumerate(kv_parts)
    ]
    for copy in copies:
        copy.start()

    token = lax.rem(lax.broadcasted_iota(jnp.int32, (rows, head_dim), 0), BLK)
    column = lax.broadcasted_iota(jnp.int32, (rows, head_dim), 1)
    masked = ((column < BLK) & (column > token)) | (column == BLK)
    qext[...] = jnp.where(masked, -BIG, 0.0).astype(jnp.bfloat16)
    key_iota = lax.broadcasted_iota(jnp.int32, (BLK, head_dim), 0)
    lane = lax.broadcasted_iota(jnp.int32, (BLK, head_dim), 1)
    etile[0] = jnp.zeros((BLK, head_dim), jnp.bfloat16)
    etile[1] = jnp.where(lane == BLK, 1.0, 0.0).astype(jnp.bfloat16)
    etile[2] = jnp.where(lane == key_iota, 1.0, 0.0).astype(jnp.bfloat16)

    for copy in copies:
        copy.wait()

    @pl.loop(0, total // BLK)
    def _(block):
        start = pl.multiple_of(block * BLK, BLK)
        value = kv[pl.ds(start, BLK), pl.ds(head_dim, head_dim)]
        vt[block] = jnp.concatenate([value, value], axis=0).T

    span = math.gcd(total, 512)
    where = vrow_ref[...]
    position = lax.broadcasted_iota(jnp.int32, (verts, span), 1)

    def select(step, found):
        start = pl.multiple_of(step * span, span)
        chosen = jnp.where(where == position + start, 1.0, 0.0).astype(jnp.bfloat16)
        return found + jnp.dot(
            chosen, kv[pl.ds(start, span), :], preferred_element_type=jnp.float32
        )

    found = lax.fori_loop(
        0, total // span, select, jnp.zeros((verts, 2 * head_dim), jnp.float32)
    ).astype(jnp.bfloat16)
    kvert[...] = found[:, :head_dim]
    vtvert[...] = found[:, head_dim:].T

    low = lax.broadcasted_iota(jnp.int32, (head_dim, 2 * BLK), 1) < BLK

    @pl.loop(0, blocks_here)
    def _(here):
        start = pl.multiple_of(here * BLK, BLK)
        query = jnp.concatenate(
            [q_ref[pl.ds(start, BLK), pl.ds(g * head_dim, head_dim)] for g in range(group)], axis=0
        )
        query = jnp.concatenate([query, qext[...]], axis=1)
        own = own_ref[0] + here

        def key_block(block):
            return kv[pl.ds(pl.multiple_of(block * BLK, BLK), BLK), pl.ds(0, head_dim)]

        def keys_of(t):
            if t == 0:
                key = key_block(own)
                left = jnp.concatenate([key, key], axis=0)
                right = jnp.concatenate([etile[2], etile[1]], axis=0)
            elif t <= listed // CHUNK:
                at = here * listed + (t - 1) * CHUNK
                left = jnp.concatenate([key_block(idx_ref[at + i]) for i in range(CHUNK)], axis=0)
                right = jnp.concatenate([etile[dead_ref[at + i]] for i in range(CHUNK)], axis=0)
            else:
                left = kvert[...]
                right = ev_ref[here]
            return jnp.concatenate([left, right], axis=1)

        def values_of(t):
            if t == 0:
                return vt[own]
            if t <= listed // CHUNK:
                at = here * listed + (t - 1) * CHUNK
                return jnp.concatenate(
                    [
                        jnp.where(low, vt[idx_ref[at + i]], vt[idx_ref[at + i + 1]])
                        for i in range(0, CHUNK, 2)
                    ],
                    axis=1,
                )
            return vtvert[...]

        tiles = listed // CHUNK + 2
        sizes = [2 * BLK] + [CHUNK * BLK] * (listed // CHUNK) + [verts]
        starts = [sum(sizes[:t]) for t in range(tiles)]
        top = jnp.full((8, rows), -jnp.inf, jnp.float32)
        for t in range(tiles):
            tile = lax.dot_general(
                keys_of(t), query, (((1,), (1,)), ((), ())), preferred_element_type=jnp.float32
            )
            scores[pl.ds(starts[t], sizes[t]), :] = tile
            top = jnp.maximum(top, jnp.max(tile.reshape(sizes[t] // 8, 8, rows), axis=0))
        top = jnp.max(top, axis=0, keepdims=True)
        weight = jnp.zeros((8, rows), jnp.float32)
        mixed = jnp.zeros((head_dim, rows), jnp.float32)
        for t in range(tiles):
            expo = jnp.exp2((scores[pl.ds(starts[t], sizes[t]), :] - top) * scale)
            weight = weight + jnp.sum(expo.reshape(sizes[t] // 8, 8, rows), axis=0)
            mixed = mixed + jnp.dot(
                values_of(t), expo.astype(jnp.bfloat16), preferred_element_type=jnp.float32
            )
        mixed = mixed / jnp.sum(weight, axis=0, keepdims=True)
        result = mixed.T.astype(jnp.bfloat16)
        for g in range(group):
            out_ref[pl.ds(start, BLK), pl.ds(g * head_dim, head_dim)] = result[
                g * BLK : (g + 1) * BLK
            ]


def attend(idx, dead, own, query, vrow, ev, kv_parts, head_dim, group, listed):
    parts = len(kv_parts)
    total = sum(part.shape[0] for part in kv_parts)
    tokens = query.shape[0]
    verts = vrow.shape[0]
    rows = BLK * group
    keys = (listed + 2) * BLK + verts
    smem = pl.BlockSpec(memory_space=pltpu.SMEM)
    vmem = pl.BlockSpec(memory_space=pltpu.VMEM)
    hbm = pl.BlockSpec(memory_space=pl.ANY)
    work = tokens * group * keys
    return pl.pallas_call(
        functools.partial(
            attention_kernel, parts=parts, listed=listed, head_dim=head_dim, group=group
        ),
        out_shape=jax.ShapeDtypeStruct((tokens, group * head_dim), jnp.bfloat16),
        in_specs=[smem, smem, smem, vmem, vmem, vmem] + [hbm] * parts,
        out_specs=vmem,
        scratch_shapes=[
            pltpu.VMEM((total, 2 * head_dim), jnp.bfloat16),
            pltpu.VMEM((total // BLK, head_dim, 2 * BLK), jnp.bfloat16),
            pltpu.VMEM((verts, head_dim), jnp.bfloat16),
            pltpu.VMEM((head_dim, verts), jnp.bfloat16),
            pltpu.VMEM((rows, head_dim), jnp.bfloat16),
            pltpu.VMEM((3, BLK, head_dim), jnp.bfloat16),
            pltpu.VMEM((keys, rows), jnp.float32),
            pltpu.SemaphoreType.DMA((parts,)),
        ],
        compiler_params=pltpu.CompilerParams(vmem_limit_bytes=48 << 20),
        cost_estimate=pl.CostEstimate(
            flops=4 * work * head_dim,
            transcendentals=work,
            bytes_accessed=total * 2 * head_dim * 2 + tokens * group * head_dim * 4,
        ),
    )(idx, dead, own, query, vrow, ev, *kv_parts)


def body(queries, keys, values, vertical, slash, *, cores, chips, heads):
    tok, q_width = queries.shape
    all_heads = vertical.shape[0] * heads
    head_dim = keys.shape[1] // all_heads
    group = q_width // keys.shape[1]
    ways = cores * heads
    mine = all_heads // ways
    listed = slash.shape[2]
    axes = ("head", "core") if cores > 1 else ("head",)
    groups = chips if cores > 1 else lax.axis_size("chip") * lax.axis_size("core")
    per_group = tok * ways // BLK
    chip = lax.axis_index("chip")
    if cores == 1:
        chip = chip * lax.axis_size("core") + lax.axis_index("core")

    swap = functools.partial(lax.all_to_all, axis_name=axes, tiled=True)
    pair = jnp.concatenate(
        [
            keys.reshape(tok, ways, mine, 1, head_dim),
            values.reshape(tok, ways, mine, 1, head_dim),
        ],
        axis=3,
    ).reshape(tok, ways * mine * 2 * head_dim)
    pair = swap(pair, split_axis=1, concat_axis=0)
    query = swap(queries, split_axis=1, concat_axis=0)

    relative = cores > 1 and chips == 8
    along = tok // BLK if cores > 1 else per_group

    def stored(local):
        if cores == 1:
            return local
        chunk, rest = local // along, local % along
        return ((chunk % heads) * cores + chunk // heads) * along + rest

    def place(block):
        source, local = block // per_group, block % per_group
        if relative:
            source = 2 * (chip // 2 - source // 2) + (chip % 2 + source % 2) % 2
        return source * per_group + stored(local)

    first = lax.axis_index("core") * mine if cores > 1 else 0
    slash = lax.dynamic_slice_in_dim(slash, first, mine, axis=0)
    vertical = lax.dynamic_slice_in_dim(vertical, first, mine, axis=0)
    lists = lax.dynamic_slice_in_dim(slash, chip * per_group, per_group, axis=1)
    ids = chip * per_group + jnp.arange(per_group, dtype=jnp.int32)
    vert_block = vertical // BLK
    covered = jnp.any(lists[:, :, :, None] == vert_block[:, None, None, :], axis=2)
    hidden = covered | (vert_block[:, None, :] >= ids[None, :, None])
    if cores > 1:
        order = lambda x: jnp.swapaxes(
            x.reshape(mine, cores, heads, along, x.shape[2]), 1, 2
        ).reshape(x.shape)
        lists, hidden = order(lists), order(hidden)
    lane = jnp.arange(head_dim, dtype=jnp.int32) == BLK
    ev = (hidden[..., None] & lane).astype(jnp.bfloat16)
    dead = (lists < 0).astype(jnp.int32)
    own = jnp.full((1,), 0 if relative else 1, jnp.int32) * chip * per_group
    idx = jnp.where(lists < 0, own, place(jnp.maximum(lists, 0)))
    vrow = place(vert_block) * BLK + vertical % BLK
    vrow = jnp.where(vert_block < chip * per_group + per_group, vrow, -1)

    results = []
    for h in range(mine):
        part = pair[:, h * 2 * head_dim : (h + 1) * 2 * head_dim]
        if relative:
            across = [(i, i ^ 1) for i in range(chips)]
            up = [(i, i + 2) for i in range(chips - 2)]
            parts = []
            for step in range(chips // 2):
                parts += [part, lax.ppermute(part, "chip", across)]
                if step + 1 < chips // 2:
                    part = lax.ppermute(part, "chip", up)
        else:
            axis = "chip" if cores > 1 else ("chip", "core")
            parts = [lax.all_gather(part, axis, axis=0, tiled=True)]
        results.append(
            attend(
                idx[h].reshape(-1),
                dead[h].reshape(-1),
                own,
                query[:, h * group * head_dim : (h + 1) * group * head_dim],
                vrow[h][:, None],
                ev[h],
                parts,
                head_dim,
                group,
                listed,
            )
        )
    out = [swap(result, split_axis=0, concat_axis=1) for result in results]
    out = jnp.stack([x.reshape(tok, ways, group * head_dim) for x in out], axis=2)
    return out.reshape(tok, q_width)


def solution(mesh):
    seq, heads = mesh.shape["seq"], mesh.shape["head"]
    split = Mesh(mesh.devices.reshape(seq // 2, 2, heads), ("chip", "core", "head"))
    spec = P(("chip", "core", "head"), None)

    def run(queries, keys, values, vertical, slash):
        local_heads = vertical.shape[0] // heads
        tok = queries.shape[0] // (seq * heads)
        cores = 2 if local_heads % 2 == 0 and tok % BLK == 0 else 1
        return jax.shard_map(
            functools.partial(body, cores=cores, chips=seq // 2, heads=heads),
            mesh=split,
            in_specs=(spec, spec, spec, P("head", None), P("head", None, None)),
            out_specs=spec,
            check_vma=False,
        )(queries, keys, values, vertical, slash)

    return run
```

```python
import functools
import math

import jax
import jax.numpy as jnp
from jax import lax
from jax.experimental import pallas as pl
from jax.experimental.pallas import tpu as pltpu
from jax.sharding import Mesh, PartitionSpec as P

BLK = 64
BIG = 1.0e30
LIVE, DEAD, OWN, PICKED = 0, 1, 2, 3
BF16, F32 = jnp.bfloat16, jnp.float32


def arrange_kernel(k_ref, v_ref, o_ref):
    width = v_ref.shape[0]
    head_dim = o_ref.shape[2] - width
    for h in range(o_ref.shape[0]):
        o_ref[h, :, :head_dim] = k_ref[:, h * head_dim : (h + 1) * head_dim]
        o_ref[h, :, head_dim:] = v_ref[:, h * head_dim : (h + 1) * head_dim].T


def arrange(keys, values, heads):
    tok, width = keys.shape
    head_dim = width // heads
    return pl.pallas_call(
        arrange_kernel,
        out_shape=jax.ShapeDtypeStruct((heads, tok, head_dim + tok), BF16),
    )(keys, values)


def step_kernel(code_ref, q_ref, pick_ref, *rest, parts, first, last, heads, head_dim, group):
    part_refs = rest[:parts]
    rest = rest[parts:]
    if first:
        acc_in = stat_in = None
    else:
        acc_in, stat_in = rest[:2]
        rest = rest[2:]
    if last:
        out_ref = rest[0]
        rest = rest[1:]
    else:
        acc_out, stat_out = rest[:2]
        rest = rest[2:]
    qext, etile, score_a, score_b = rest
    rows = BLK * group
    chunks, _, wide, _ = part_refs[0].shape
    per_chunk = wide // BLK
    per_part = chunks * per_chunk
    slots = parts * per_part
    blocks_here = q_ref.shape[0] * q_ref.shape[1] // BLK
    scale = math.log2(math.e) / math.sqrt(head_dim)

    token = lax.rem(lax.broadcasted_iota(jnp.int32, (rows, head_dim), 0), BLK)
    column = lax.broadcasted_iota(jnp.int32, (rows, head_dim), 1)
    masked = ((column < BLK) & (column > token)) | (column == BLK)
    qext[...] = jnp.where(masked, -BIG, 0.0).astype(BF16)
    key_iota = lax.broadcasted_iota(jnp.int32, (BLK, head_dim), 0)
    lane = lax.broadcasted_iota(jnp.int32, (BLK, head_dim), 1)
    etile[LIVE] = jnp.zeros((BLK, head_dim), BF16)
    etile[DEAD] = jnp.where(lane == BLK, 1.0, 0.0).astype(BF16)
    etile[OWN] = jnp.where(lane == key_iota, 1.0, 0.0).astype(BF16)

    def pair_loop(h):
        for slot in range(slots):
            etile[PICKED + slot] = pick_ref[h, slot]

        def scored(here, buffer):
            chunk = here // per_q
            start = pl.multiple_of(lax.rem(here, per_q) * BLK, BLK)
            query = jnp.concatenate(
                [
                    q_ref[chunk, pl.ds(start, BLK), pl.ds((h * group + g) * head_dim, head_dim)]
                    for g in range(group)
                ],
                axis=0,
            )
            query = jnp.concatenate([query, qext[...]], axis=1)
            at = (h * blocks_here + here) * slots
            top = jnp.full((8, rows), -jnp.inf, F32)
            size = per_part * BLK
            for p, part in enumerate(part_refs):
                left = [part[c, h, :, pl.ds(0, head_dim)] for c in range(chunks)]
                right = [etile[code_ref[at + p * per_part + i]] for i in range(per_part)]
                key = jnp.concatenate(
                    [jnp.concatenate(left, axis=0), jnp.concatenate(right, axis=0)], axis=1
                )
                tile = lax.dot_general(
                    key, query, (((1,), (1,)), ((), ())), preferred_element_type=F32
                )
                buffer[pl.ds(p * size, size), :] = tile
                top = jnp.maximum(top, jnp.max(tile.reshape(size // 8, 8, rows), axis=0))
            return jnp.max(top, axis=0, keepdims=True)

        def mixed_in(here, buffer, top):
            pair = h * blocks_here + here
            if first:
                top = jnp.broadcast_to(top, (8, rows))
                weight = jnp.zeros((8, rows), F32)
            else:
                before = stat_in[pair, :8]
                top = jnp.maximum(top, before)
                fade = jnp.exp2((before - top) * scale)
                weight = stat_in[pair, 8:] * fade
            mixed = jnp.zeros((head_dim, rows), F32)
            size = per_part * BLK
            for p, part in enumerate(part_refs):
                tile = buffer[pl.ds(p * size, size), :].reshape(size // 8, 8, rows)
                expo = jnp.exp2((tile - top[None]) * scale)
                weight = weight + jnp.sum(expo, axis=0)
                value = jnp.concatenate(
                    [part[c, h, :, pl.ds(head_dim, wide)] for c in range(chunks)], axis=1
                )
                mixed = mixed + jnp.dot(
                    value, expo.reshape(size, rows).astype(BF16), preferred_element_type=F32
                )
            if not first:
                mixed = mixed + acc_in[pair] * fade[:1]
            if not last:
                acc_out[pair] = mixed
                stat_out[pair, :8] = top
                stat_out[pair, 8:] = weight
                return
            result = (mixed / jnp.sum(weight, axis=0, keepdims=True)).T.astype(BF16)
            chunk = here // per_q
            start = pl.multiple_of(lax.rem(here, per_q) * BLK, BLK)
            for g in range(group):
                out_ref[chunk, pl.ds(start, BLK), pl.ds((h * group + g) * head_dim, head_dim)] = (
                    result[g * BLK : (g + 1) * BLK]
                )

        per_q = q_ref.shape[1] // BLK

        @pl.loop(0, blocks_here // 2)
        def _(step):
            top_a = scored(2 * step, score_a)
            top_b = scored(2 * step + 1, score_b)
            mixed_in(2 * step, score_a, top_a)
            mixed_in(2 * step + 1, score_b, top_b)

    for h in range(heads):
        pair_loop(h)


def attend_step(code, query, pick, parts, state, last, head_dim, group):
    heads = pick.shape[0]
    slots = pick.shape[1]
    blocks_here = query.shape[0] * query.shape[1] // BLK
    rows = BLK * group
    pairs = heads * blocks_here
    first = state is None
    smem = pl.BlockSpec(memory_space=pltpu.SMEM)
    vmem = pl.BlockSpec(memory_space=pltpu.VMEM)
    state_shape = (
        jax.ShapeDtypeStruct((pairs, head_dim, rows), F32),
        jax.ShapeDtypeStruct((pairs, 16, rows), F32),
    )
    state = () if first else tuple(state)
    work = pairs * rows * slots * BLK
    return pl.pallas_call(
        functools.partial(
            step_kernel,
            parts=len(parts),
            first=first,
            last=last,
            heads=heads,
            head_dim=head_dim,
            group=group,
        ),
        out_shape=jax.ShapeDtypeStruct(query.shape, BF16) if last else state_shape,
        in_specs=[smem] + [vmem] * (2 + len(parts) + len(state)),
        out_specs=vmem if last else (vmem, vmem),
        scratch_shapes=[
            pltpu.VMEM((rows, head_dim), BF16),
            pltpu.VMEM((PICKED + slots, BLK, head_dim), BF16),
            pltpu.VMEM((slots * BLK, rows), F32),
            pltpu.VMEM((slots * BLK, rows), F32),
        ],
        compiler_params=pltpu.CompilerParams(vmem_limit_bytes=40 << 20),
        cost_estimate=pl.CostEstimate(
            flops=4 * work * head_dim,
            transcendentals=work,
            bytes_accessed=8 << 20,
        ),
    )(code, query, pick, *parts, *state)


def body(queries, keys, values, vertical, slash, *, cores, chips, heads):
    tok, q_width = queries.shape
    all_heads = vertical.shape[0] * heads
    head_dim = keys.shape[1] // all_heads
    group = q_width // keys.shape[1]
    ways = cores * heads
    mine = all_heads // ways
    axes = ("head", "core") if cores > 1 else ("head",)
    groups = chips if cores > 1 else chips * 2
    per_group = tok * ways // BLK
    chip = lax.axis_index("chip")
    if cores == 1:
        chip = chip * 2 + lax.axis_index("core")
    relative = cores > 1 and chips == 8
    swap = functools.partial(
        lax.all_to_all, axis_name=axes, split_axis=0, concat_axis=0, tiled=True
    )

    if relative:
        pair = swap(arrange(keys, values, all_heads).reshape(ways, mine, tok, head_dim + tok))
    else:
        pair = jnp.concatenate(
            [keys.reshape(tok, ways, mine, head_dim), values.reshape(tok, ways, mine, head_dim)],
            axis=3,
        )
        pair = swap(pair.transpose(1, 2, 0, 3))
    query = swap(queries.reshape(tok, ways, q_width // ways).transpose(1, 0, 2))
    query = query.reshape(-1, max(tok, BLK), q_width // ways)

    along = tok // BLK
    local = jnp.arange(per_group, dtype=jnp.int32)
    if cores > 1:
        local = local.reshape(cores, heads, along).swapaxes(0, 1).reshape(-1)
    first_head = lax.axis_index("core") * mine if cores > 1 else 0
    slash = lax.dynamic_slice_in_dim(slash, first_head, mine, axis=0)
    vertical = lax.dynamic_slice_in_dim(vertical, first_head, mine, axis=0)
    lists = lax.dynamic_slice_in_dim(slash, chip * per_group, per_group, axis=1)
    if cores > 1:
        lists = (
            lists.reshape(mine, cores, heads, along, -1).swapaxes(1, 2).reshape(lists.shape)
        )
    ids = chip * per_group + local

    if relative:
        across = [(i, i ^ 1) for i in range(chips)]
        up = [(i, i + 2) for i in range(chips - 2)]
        steps = []
        part = pair
        for step in range(chips // 2):
            later = lax.ppermute(part, "chip", up) if step + 1 < chips // 2 else None
            other = lax.ppermute(part, "chip", across)
            source = chip // 2 - step
            col = jnp.stack([chip % 2, 1 - chip % 2])
            source = jnp.where(source < 0, groups, 2 * source + col)
            steps.append(((part, other), source))
            part = later
    else:
        axis = "chip" if cores > 1 else ("chip", "core")
        rows = pair.transpose(1, 0, 2, 3).reshape(mine, -1, 2 * head_dim)
        rows = lax.all_gather(rows, axis, axis=1, tiled=True)
        pieces = rows.shape[1] // (2 * BLK)
        turned = rows[..., head_dim:].reshape(mine, pieces, 2 * BLK, head_dim).swapaxes(2, 3)
        rows = rows[..., :head_dim].reshape(mine, pieces, 2 * BLK, head_dim)
        rows = jnp.concatenate([rows, turned], axis=3).swapaxes(0, 1)
        each = per_group // 2
        order = (chip + jnp.arange(groups, dtype=jnp.int32)) % groups
        rows = jnp.roll(rows.reshape((groups, each) + rows.shape[1:]), -chip, axis=0)
        many = math.gcd(groups, 4)
        steps = [
            ((rows[g : g + many].reshape((many * each,) + rows.shape[2:]),), order[g : g + many])
            for g in range(0, groups, many)
        ]

    state = None
    for n, (parts, source) in enumerate(steps):
        nat = (source[:, None] * per_group + local).reshape(-1)
        listed = jnp.any(lists[:, :, :, None] == nat, axis=2)
        slot = PICKED + jnp.arange(nat.shape[0], dtype=jnp.int32)
        code = jnp.where(
            listed,
            LIVE,
            jnp.where(nat == ids[:, None], OWN, jnp.where(nat > ids[:, None], DEAD, slot)),
        )
        position = nat[:, None] * BLK + jnp.arange(BLK, dtype=jnp.int32)
        hidden = jnp.all(vertical[:, None, None, :] != position[..., None], axis=3)
        lane = jnp.arange(head_dim, dtype=jnp.int32) == BLK
        pick = (hidden[..., None] & lane).astype(BF16)
        state = attend_step(
            code.reshape(-1), query, pick, parts, state, n + 1 == len(steps), head_dim, group
        )
    out = swap(state.reshape(ways, tok, q_width // ways))
    return out.transpose(1, 0, 2).reshape(tok, q_width)


def solution(mesh):
    seq, heads = mesh.shape["seq"], mesh.shape["head"]
    split = Mesh(mesh.devices.reshape(seq // 2, 2, heads), ("chip", "core", "head"))
    spec = P(("chip", "core", "head"), None)

    def run(queries, keys, values, vertical, slash):
        local_heads = vertical.shape[0] // heads
        tok = queries.shape[0] // (seq * heads)
        cores = 2 if local_heads % 2 == 0 and tok % BLK == 0 else 1
        return jax.shard_map(
            functools.partial(body, cores=cores, chips=seq // 2, heads=heads),
            mesh=split,
            in_specs=(spec, spec, spec, P("head", None), P("head", None, None)),
            out_specs=spec,
            check_vma=False,
        )(queries, keys, values, vertical, slash)

    return run
```

```python
import functools
import math

import jax
import jax.numpy as jnp
from jax import lax
from jax.experimental import pallas as pl
from jax.experimental.pallas import tpu as pltpu
from jax.sharding import Mesh, PartitionSpec as P

BLK = 64
BIG = 1.0e30
LIVE, DEAD, OWN, PICKED = 0, 1, 2, 3
BF16, F32 = jnp.bfloat16, jnp.float32


def arrange_kernel(k_ref, v_ref, o_ref):
    width = v_ref.shape[0]
    head_dim = o_ref.shape[2] - width
    for h in range(o_ref.shape[0]):
        o_ref[h, :, :head_dim] = k_ref[:, h * head_dim : (h + 1) * head_dim]
        o_ref[h, :, head_dim:] = v_ref[:, h * head_dim : (h + 1) * head_dim].T


def arrange(keys, values, heads):
    tok, width = keys.shape
    head_dim = width // heads
    return pl.pallas_call(
        arrange_kernel,
        out_shape=jax.ShapeDtypeStruct((heads, tok, head_dim + tok), BF16),
    )(keys, values)


def step_kernel(code_ref, q_ref, pick_ref, *rest, parts, first, last, span, head_dim, group):
    part_refs, rest = rest[:parts], rest[parts:]
    if not first:
        (acc_in, stat_in, _), rest = rest[:3], rest[3:]
    if last:
        out_ref, rest = rest[0], rest[1:]
    else:
        (acc_out, stat_out, mark_out), rest = rest[:3], rest[3:]
        mark_out[...] = jnp.zeros(mark_out.shape, BF16)
    qext, etile, score_a, score_b = rest
    rows = BLK * group
    chunks, _, wide, _ = part_refs[0].shape
    per_part = chunks * wide // BLK
    slots = parts * per_part
    size = per_part * BLK
    per_q = q_ref.shape[1] // BLK
    blocks_here = q_ref.shape[0] * per_q
    scale = math.log2(math.e) / math.sqrt(head_dim)

    token = lax.rem(lax.broadcasted_iota(jnp.int32, (rows, head_dim), 0), BLK)
    column = lax.broadcasted_iota(jnp.int32, (rows, head_dim), 1)
    masked = ((column < BLK) & (column > token)) | (column == BLK)
    qext[...] = jnp.where(masked, -BIG, 0.0).astype(BF16)
    key_iota = lax.broadcasted_iota(jnp.int32, (BLK, head_dim), 0)
    lane = lax.broadcasted_iota(jnp.int32, (BLK, head_dim), 1)
    etile[LIVE] = jnp.zeros((BLK, head_dim), BF16)
    etile[DEAD] = jnp.where(lane == BLK, 1.0, 0.0).astype(BF16)
    etile[OWN] = jnp.where(lane == key_iota, 1.0, 0.0).astype(BF16)

    def place(here, g):
        start = pl.multiple_of(lax.rem(here, per_q) * BLK, BLK)
        return lax.div(here, per_q), pl.ds(start, BLK), pl.ds(g * head_dim, head_dim)

    def scored(head, here, buffer):
        query = jnp.concatenate(
            [q_ref[place(here, head * group + g)] for g in range(group)], axis=0
        )
        query = jnp.concatenate([query, qext[...]], axis=1)
        top = jnp.full((8, rows), -jnp.inf, F32)
        for p, part in enumerate(part_refs):
            left = [part[c, head, :, pl.ds(0, head_dim)] for c in range(chunks)]
            right = [
                etile[code_ref[head, here, p * per_part + i]] for i in range(per_part)
            ]
            key = jnp.concatenate(
                [jnp.concatenate(left, axis=0), jnp.concatenate(right, axis=0)], axis=1
            )
            tile = lax.dot_general(
                key, query, (((1,), (1,)), ((), ())), preferred_element_type=F32
            )
            buffer[pl.ds(p * size, size), :] = tile
            top = jnp.maximum(top, jnp.max(tile.reshape(size // 8, 8, rows), axis=0))
        return jnp.max(top, axis=0, keepdims=True)

    def mixed_in(head, here, buffer, top):
        at = head * blocks_here + here
        if first:
            top = jnp.broadcast_to(top, (8, rows))
            weight = jnp.zeros((8, rows), F32)
        else:
            before = stat_in[at, :8]
            top = jnp.maximum(top, before)
            fade = jnp.exp2((before - top) * scale)
            weight = stat_in[at, 8:] * fade
        mixed = jnp.zeros((head_dim, rows), F32)
        for p, part in enumerate(part_refs):
            tile = buffer[pl.ds(p * size, size), :].reshape(size // 8, 8, rows)
            expo = jnp.exp2((tile - top[None]) * scale)
            weight = weight + jnp.sum(expo, axis=0)
            value = jnp.concatenate(
                [part[c, head, :, pl.ds(head_dim, wide)] for c in range(chunks)], axis=1
            )
            mixed = mixed + jnp.dot(
                value, expo.reshape(size, rows).astype(BF16), preferred_element_type=F32
            )
        if not first:
            mixed = mixed + acc_in[at] * fade[:1]
        if not last:
            acc_out[at] = mixed
            stat_out[at, :8] = top
            stat_out[at, 8:] = weight
            return
        result = (mixed / jnp.sum(weight, axis=0, keepdims=True)).T.astype(BF16)
        for g in range(group):
            out_ref[place(here, (head - span[0]) * group + g)] = result[g * BLK : (g + 1) * BLK]

    for head in range(*span):
        for slot in range(slots):
            etile[PICKED + slot] = pick_ref[head, slot]

        @pl.loop(0, blocks_here // 2)
        def _(step):
            top_a = scored(head, 2 * step, score_a)
            top_b = scored(head, 2 * step + 1, score_b)
            mixed_in(head, 2 * step, score_a, top_a)
            mixed_in(head, 2 * step + 1, score_b, top_b)


def attend_step(code, query, pick, parts, state, span, last, head_dim, group):
    heads, slots = pick.shape[:2]
    blocks_here = query.shape[0] * query.shape[1] // BLK
    rows = BLK * group
    smem = pl.BlockSpec(memory_space=pltpu.SMEM)
    vmem = pl.BlockSpec(memory_space=pltpu.VMEM)
    carried = (
        jax.ShapeDtypeStruct((heads * blocks_here, head_dim, rows), F32),
        jax.ShapeDtypeStruct((heads * blocks_here, 16, rows), F32),
        jax.ShapeDtypeStruct((16, 128), BF16),
    )
    count = span[1] - span[0]
    out = jax.ShapeDtypeStruct(query.shape[:2] + (count * group * head_dim,), BF16)
    first = state is None
    state = () if first else tuple(state)
    work = count * blocks_here * rows * slots * BLK
    return pl.pallas_call(
        functools.partial(
            step_kernel,
            parts=len(parts),
            first=first,
            last=last,
            span=span,
            head_dim=head_dim,
            group=group,
        ),
        out_shape=out if last else carried,
        in_specs=[smem] + [vmem] * (2 + len(parts) + len(state)),
        out_specs=vmem if last else (vmem,) * 3,
        scratch_shapes=[
            pltpu.VMEM((rows, head_dim), BF16),
            pltpu.VMEM((PICKED + slots, BLK, head_dim), BF16),
            pltpu.VMEM((slots * BLK, rows), F32),
            pltpu.VMEM((slots * BLK, rows), F32),
        ],
        compiler_params=pltpu.CompilerParams(vmem_limit_bytes=16 << 20),
        cost_estimate=pl.CostEstimate(
            flops=4 * work * head_dim, transcendentals=work, bytes_accessed=8 << 20
        ),
    )(code, query, pick, *parts, *state)


def body(queries, keys, values, vertical, slash, *, cores, chips, heads):
    tok, q_width = queries.shape
    all_heads = vertical.shape[0] * heads
    head_dim = keys.shape[1] // all_heads
    group = q_width // keys.shape[1]
    ways = cores * heads
    mine = all_heads // ways
    axes = ("head", "core") if cores > 1 else ("head",)
    groups = chips if cores > 1 else chips * 2
    per_group = tok * ways // BLK
    chip = lax.axis_index("chip")
    if cores == 1:
        chip = chip * 2 + lax.axis_index("core")
    relative = cores > 1 and chips == 8
    swap = functools.partial(
        lax.all_to_all, axis_name=axes, split_axis=0, concat_axis=0, tiled=True
    )

    if relative:
        pair = swap(arrange(keys, values, all_heads).reshape(ways, mine, tok, head_dim + tok))
    else:
        pair = jnp.concatenate(
            [keys.reshape(tok, ways, mine, head_dim), values.reshape(tok, ways, mine, head_dim)],
            axis=3,
        )
        pair = swap(pair.transpose(1, 2, 0, 3))
    query = swap(queries.reshape(tok, ways, q_width // ways).transpose(1, 0, 2))
    query = query.reshape(-1, max(tok, BLK), q_width // ways)

    pair, vertical, slash = lax.optimization_barrier((pair, vertical, slash))

    along = tok // BLK
    local = jnp.arange(per_group, dtype=jnp.int32)
    if cores > 1:
        local = local.reshape(cores, heads, along).swapaxes(0, 1).reshape(-1)
    first_head = lax.axis_index("core") * mine if cores > 1 else 0
    slash = lax.dynamic_slice_in_dim(slash, first_head, mine, axis=0)
    vertical = lax.dynamic_slice_in_dim(vertical, first_head, mine, axis=0)
    lists = lax.dynamic_slice_in_dim(slash, chip * per_group, per_group, axis=1)
    if cores > 1:
        lists = (
            lists.reshape(mine, cores, heads, along, -1).swapaxes(1, 2).reshape(lists.shape)
        )
    ids = chip * per_group + local

    def masks(source):
        nat = (source[:, None] * per_group + local).reshape(-1)
        listed = jnp.any(lists[:, :, :, None] == nat, axis=2)
        slot = PICKED + jnp.arange(nat.shape[0], dtype=jnp.int32)
        code = jnp.where(
            listed,
            LIVE,
            jnp.where(nat == ids[:, None], OWN, jnp.where(nat > ids[:, None], DEAD, slot)),
        )
        position = nat[:, None] * BLK + jnp.arange(BLK, dtype=jnp.int32)
        hidden = jnp.all(vertical[:, None, None, :] != position[..., None], axis=3)
        lane = jnp.arange(head_dim, dtype=jnp.int32) == BLK
        return code, (hidden[..., None] & lane).astype(BF16)

    def attend(table, parts, state, last):
        state = None if state is None else tuple(state)
        run = functools.partial(attend_step, table[0], query, table[1], parts, state)
        if not last:
            return run((0, mine), False, head_dim, group)
        return run((0, mine), True, head_dim, group)

    state = None
    if relative:
        across = [(i, i ^ 1) for i in range(chips)]
        up = [(i, i + 2) for i in range(chips - 2)]
        final = chips // 2 - 1
        col = jnp.stack([chip % 2, 1 - chip % 2])
        tables = []
        for n in range(final + 1):
            row = chip // 2 - n
            tables.append(masks(jnp.where(row < 0, groups, 2 * row + col)))
        tables = lax.optimization_barrier(tables)
        part, waiting = pair, None
        for n in range(final + 2):
            fetched = None
            if n <= final:
                if state is not None:
                    part, mark = lax.optimization_barrier((part, state[2]))
                    state = state[:2] + (mark,)
                fetched = (part, lax.ppermute(part, "chip", across))
                part = lax.ppermute(part, "chip", up) if n < final else None
            if n:
                state = attend(tables[n - 1], waiting, state, n > final)
            waiting = fetched
    else:
        axis = "chip" if cores > 1 else ("chip", "core")
        rows = pair.transpose(1, 0, 2, 3).reshape(mine, -1, 2 * head_dim)
        rows = lax.all_gather(rows, axis, axis=1, tiled=True)
        pieces = rows.shape[1] // (2 * BLK)
        turned = rows[..., head_dim:].reshape(mine, pieces, 2 * BLK, head_dim).swapaxes(2, 3)
        rows = rows[..., :head_dim].reshape(mine, pieces, 2 * BLK, head_dim)
        rows = jnp.concatenate([rows, turned], axis=3).swapaxes(0, 1)
        each = per_group // 2
        order = (chip + jnp.arange(groups, dtype=jnp.int32)) % groups
        rows = jnp.roll(rows.reshape((groups, each) + rows.shape[1:]), -chip, axis=0)
        many = math.gcd(groups, 4)
        for g in range(0, groups, many):
            part = rows[g : g + many].reshape((many * each,) + rows.shape[2:])
            state = attend(masks(order[g : g + many]), (part,), state, g + many == groups)

    out = swap(state.reshape(ways, tok, q_width // ways))
    return out.transpose(1, 0, 2).reshape(tok, q_width)


def solution(mesh):
    seq, heads = mesh.shape["seq"], mesh.shape["head"]
    split = Mesh(mesh.devices.reshape(seq // 2, 2, heads), ("chip", "core", "head"))
    spec = P(("chip", "core", "head"), None)

    def run(queries, keys, values, vertical, slash):
        local_heads = vertical.shape[0] // heads
        tok = queries.shape[0] // (seq * heads)
        cores = 2 if local_heads % 2 == 0 and tok % BLK == 0 else 1
        return jax.shard_map(
            functools.partial(body, cores=cores, chips=seq // 2, heads=heads),
            mesh=split,
            in_specs=(spec, spec, spec, P("head", None), P("head", None, None)),
            out_specs=spec,
            check_vma=False,
        )(queries, keys, values, vertical, slash)

    return run
```

```python
import functools
import math

import jax
import jax.numpy as jnp
from jax import lax
from jax.experimental import pallas as pl
from jax.experimental.pallas import tpu as pltpu
from jax.sharding import Mesh, PartitionSpec as P

BLK = 64
BIG = 1.0e30
LIVE, DEAD, OWN, PICKED = 0, 1, 2, 3
BF16, F32 = jnp.bfloat16, jnp.float32


def arrange_kernel(k_ref, v_ref, o_ref):
    width = v_ref.shape[0]
    head_dim = o_ref.shape[2] - width
    for h in range(o_ref.shape[0]):
        o_ref[h, :, :head_dim] = k_ref[:, h * head_dim : (h + 1) * head_dim]
        o_ref[h, :, head_dim:] = v_ref[:, h * head_dim : (h + 1) * head_dim].T


def arrange(keys, values, heads):
    tok, width = keys.shape
    head_dim = width // heads
    return pl.pallas_call(
        arrange_kernel,
        out_shape=jax.ShapeDtypeStruct((heads, tok, head_dim + tok), BF16),
    )(keys, values)


def step_kernel(code_ref, q_ref, pick_ref, *rest, parts, first, last, span, head_dim, group):
    part_refs, rest = rest[:parts], rest[parts:]
    if not first:
        (acc_in, stat_in, _), rest = rest[:3], rest[3:]
    if last:
        out_ref, rest = rest[0], rest[1:]
    else:
        (acc_out, stat_out, mark_out), rest = rest[:3], rest[3:]
        mark_out[...] = jnp.zeros(mark_out.shape, BF16)
    qext, etile, score_a, score_b = rest
    rows = BLK * group
    chunks, _, wide, _ = part_refs[0].shape
    per_part = chunks * wide // BLK
    slots = parts * per_part
    size = per_part * BLK
    per_q = q_ref.shape[1] // BLK
    blocks_here = q_ref.shape[0] * per_q
    scale = math.log2(math.e) / math.sqrt(head_dim)

    token = lax.rem(lax.broadcasted_iota(jnp.int32, (rows, head_dim), 0), BLK)
    column = lax.broadcasted_iota(jnp.int32, (rows, head_dim), 1)
    masked = ((column < BLK) & (column > token)) | (column == BLK)
    qext[...] = jnp.where(masked, -BIG, 0.0).astype(BF16)
    key_iota = lax.broadcasted_iota(jnp.int32, (BLK, head_dim), 0)
    lane = lax.broadcasted_iota(jnp.int32, (BLK, head_dim), 1)
    etile[LIVE] = jnp.zeros((BLK, head_dim), BF16)
    etile[DEAD] = jnp.where(lane == BLK, 1.0, 0.0).astype(BF16)
    etile[OWN] = jnp.where(lane == key_iota, 1.0, 0.0).astype(BF16)

    def place(here, g):
        start = pl.multiple_of(lax.rem(here, per_q) * BLK, BLK)
        return lax.div(here, per_q), pl.ds(start, BLK), pl.ds(g * head_dim, head_dim)

    def scored(head, here, buffer):
        query = jnp.concatenate(
            [q_ref[place(here, head * group + g)] for g in range(group)], axis=0
        )
        query = jnp.concatenate([query, qext[...]], axis=1)
        top = jnp.full((8, rows), -jnp.inf, F32)
        for p, part in enumerate(part_refs):
            left = [part[c, head, :, pl.ds(0, head_dim)] for c in range(chunks)]
            right = [
                etile[code_ref[head, here, p * per_part + i]] for i in range(per_part)
            ]
            key = jnp.concatenate(
                [jnp.concatenate(left, axis=0), jnp.concatenate(right, axis=0)], axis=1
            )
            tile = lax.dot_general(
                key, query, (((1,), (1,)), ((), ())), preferred_element_type=F32
            )
            buffer[pl.ds(p * size, size), :] = tile
            top = jnp.maximum(top, jnp.max(tile.reshape(size // 8, 8, rows), axis=0))
        return jnp.max(top, axis=0, keepdims=True)

    def mixed_in(head, here, buffer, top):
        at = head * blocks_here + here
        if first:
            top = jnp.broadcast_to(top, (8, rows))
            weight = jnp.zeros((8, rows), F32)
        else:
            before = stat_in[at, :8]
            top = jnp.maximum(top, before)
            fade = jnp.exp2((before - top) * scale)
            weight = stat_in[at, 8:] * fade
        mixed = jnp.zeros((head_dim, rows), F32)
        for p, part in enumerate(part_refs):
            tile = buffer[pl.ds(p * size, size), :].reshape(size // 8, 8, rows)
            expo = jnp.exp2((tile - top[None]) * scale)
            weight = weight + jnp.sum(expo, axis=0)
            value = jnp.concatenate(
                [part[c, head, :, pl.ds(head_dim, wide)] for c in range(chunks)], axis=1
            )
            mixed = mixed + jnp.dot(
                value, expo.reshape(size, rows).astype(BF16), preferred_element_type=F32
            )
        if not first:
            mixed = mixed + acc_in[at] * fade[:1]
        if not last:
            acc_out[at] = mixed
            stat_out[at, :8] = top
            stat_out[at, 8:] = weight
            return
        result = (mixed / jnp.sum(weight, axis=0, keepdims=True)).T.astype(BF16)
        for g in range(group):
            out_ref[place(here, (head - span[0]) * group + g)] = result[g * BLK : (g + 1) * BLK]

    for head in range(*span):
        for slot in range(slots):
            etile[PICKED + slot] = pick_ref[head, slot]

        @pl.loop(0, blocks_here // 2)
        def _(step):
            top_a = scored(head, 2 * step, score_a)
            top_b = scored(head, 2 * step + 1, score_b)
            mixed_in(head, 2 * step, score_a, top_a)
            mixed_in(head, 2 * step + 1, score_b, top_b)


def attend_step(code, query, pick, parts, state, span, last, head_dim, group):
    heads, slots = pick.shape[:2]
    blocks_here = query.shape[0] * query.shape[1] // BLK
    rows = BLK * group
    smem = pl.BlockSpec(memory_space=pltpu.SMEM)
    vmem = pl.BlockSpec(memory_space=pltpu.VMEM)
    carried = (
        jax.ShapeDtypeStruct((heads * blocks_here, head_dim, rows), F32),
        jax.ShapeDtypeStruct((heads * blocks_here, 16, rows), F32),
        jax.ShapeDtypeStruct((16, 128), BF16),
    )
    count = span[1] - span[0]
    out = jax.ShapeDtypeStruct(query.shape[:2] + (count * group * head_dim,), BF16)
    first = state is None
    state = () if first else tuple(state)
    work = count * blocks_here * rows * slots * BLK
    return pl.pallas_call(
        functools.partial(
            step_kernel,
            parts=len(parts),
            first=first,
            last=last,
            span=span,
            head_dim=head_dim,
            group=group,
        ),
        out_shape=out if last else carried,
        in_specs=[smem] + [vmem] * (2 + len(parts) + len(state)),
        out_specs=vmem if last else (vmem,) * 3,
        scratch_shapes=[
            pltpu.VMEM((rows, head_dim), BF16),
            pltpu.VMEM((PICKED + slots, BLK, head_dim), BF16),
            pltpu.VMEM((slots * BLK, rows), F32),
            pltpu.VMEM((slots * BLK, rows), F32),
        ],
        compiler_params=pltpu.CompilerParams(vmem_limit_bytes=16 << 20),
        cost_estimate=pl.CostEstimate(
            flops=4 * work * head_dim, transcendentals=work, bytes_accessed=8 << 20
        ),
    )(code, query, pick, *parts, *state)


def body(queries, keys, values, vertical, slash, *, cores, chips, heads):
    tok, q_width = queries.shape
    all_heads = vertical.shape[0] * heads
    head_dim = keys.shape[1] // all_heads
    group = q_width // keys.shape[1]
    ways = cores * heads
    mine = all_heads // ways
    axes = ("head", "core") if cores > 1 else ("head",)
    groups = chips if cores > 1 else chips * 2
    per_group = tok * ways // BLK
    chip = lax.axis_index("chip")
    if cores == 1:
        chip = chip * 2 + lax.axis_index("core")
    relative = cores > 1 and chips == 8
    swap = functools.partial(
        lax.all_to_all, axis_name=axes, split_axis=0, concat_axis=0, tiled=True
    )

    if relative:
        pair = swap(arrange(keys, values, all_heads).reshape(ways, mine, tok, head_dim + tok))
    else:
        pair = jnp.concatenate(
            [keys.reshape(tok, ways, mine, head_dim), values.reshape(tok, ways, mine, head_dim)],
            axis=3,
        )
        pair = swap(pair.transpose(1, 2, 0, 3))
    query = queries.reshape(tok, ways, q_width // ways).transpose(1, 0, 2)

    pair, vertical, slash = lax.optimization_barrier((pair, vertical, slash))

    along = tok // BLK
    local = jnp.arange(per_group, dtype=jnp.int32)
    if cores > 1:
        local = local.reshape(cores, heads, along).swapaxes(0, 1).reshape(-1)
    first_head = lax.axis_index("core") * mine if cores > 1 else 0
    slash = lax.dynamic_slice_in_dim(slash, first_head, mine, axis=0)
    vertical = lax.dynamic_slice_in_dim(vertical, first_head, mine, axis=0)
    lists = lax.dynamic_slice_in_dim(slash, chip * per_group, per_group, axis=1)
    if cores > 1:
        lists = (
            lists.reshape(mine, cores, heads, along, -1).swapaxes(1, 2).reshape(lists.shape)
        )
    ids = chip * per_group + local

    def masks(source):
        nat = (source[:, None] * per_group + local).reshape(-1)
        listed = jnp.any(lists[:, :, :, None] == nat, axis=2)
        slot = PICKED + jnp.arange(nat.shape[0], dtype=jnp.int32)
        code = jnp.where(
            listed,
            LIVE,
            jnp.where(nat == ids[:, None], OWN, jnp.where(nat > ids[:, None], DEAD, slot)),
        )
        position = nat[:, None] * BLK + jnp.arange(BLK, dtype=jnp.int32)
        hidden = jnp.all(vertical[:, None, None, :] != position[..., None], axis=3)
        lane = jnp.arange(head_dim, dtype=jnp.int32) == BLK
        return code, (hidden[..., None] & lane).astype(BF16)

    def attend(query, table, parts, state, last):
        state = None if state is None else tuple(state)
        run = functools.partial(attend_step, table[0], query, table[1], parts, state)
        if not last:
            return run((0, mine), False, head_dim, group)
        return run((0, mine), True, head_dim, group)

    state = None
    if relative:
        across = [(i, i ^ 1) for i in range(chips)]
        up = [(i, i + 2) for i in range(chips - 2)]
        final = chips // 2 - 1
        col = jnp.stack([chip % 2, 1 - chip % 2])
        tables = []
        for n in range(final + 1):
            row = chip // 2 - n
            tables.append(masks(jnp.where(row < 0, groups, 2 * row + col)))
        code, query = lax.optimization_barrier((tables[0][0], query))
        tables[0] = (code, tables[0][1])
        query = swap(query).reshape(-1, max(tok, BLK), q_width // ways)
        part, waiting = pair, None
        for n in range(final + 2):
            fetched = None
            if n <= final:
                if n == 1:
                    part, tables = lax.optimization_barrier((part, tables))
                if state is not None:
                    part, mark = lax.optimization_barrier((part, state[2]))
                    state = state[:2] + (mark,)
                fetched = (part, lax.ppermute(part, "chip", across))
                part = lax.ppermute(part, "chip", up) if n < final else None
            if n:
                state = attend(query, tables[n - 1], waiting, state, n > final)
            waiting = fetched
    else:
        query = swap(query).reshape(-1, max(tok, BLK), q_width // ways)
        axis = "chip" if cores > 1 else ("chip", "core")
        rows = pair.transpose(1, 0, 2, 3).reshape(mine, -1, 2 * head_dim)
        rows = lax.all_gather(rows, axis, axis=1, tiled=True)
        pieces = rows.shape[1] // (2 * BLK)
        turned = rows[..., head_dim:].reshape(mine, pieces, 2 * BLK, head_dim).swapaxes(2, 3)
        rows = rows[..., :head_dim].reshape(mine, pieces, 2 * BLK, head_dim)
        rows = jnp.concatenate([rows, turned], axis=3).swapaxes(0, 1)
        each = per_group // 2
        order = (chip + jnp.arange(groups, dtype=jnp.int32)) % groups
        rows = jnp.roll(rows.reshape((groups, each) + rows.shape[1:]), -chip, axis=0)
        many = math.gcd(groups, 4)
        for g in range(0, groups, many):
            part = rows[g : g + many].reshape((many * each,) + rows.shape[2:])
            state = attend(query, masks(order[g : g + many]), (part,), state, g + many == groups)

    out = swap(state.reshape(ways, tok, q_width // ways))
    return out.transpose(1, 0, 2).reshape(tok, q_width)


def solution(mesh):
    seq, heads = mesh.shape["seq"], mesh.shape["head"]
    split = Mesh(mesh.devices.reshape(seq // 2, 2, heads), ("chip", "core", "head"))
    spec = P(("chip", "core", "head"), None)

    def run(queries, keys, values, vertical, slash):
        local_heads = vertical.shape[0] // heads
        tok = queries.shape[0] // (seq * heads)
        cores = 2 if local_heads % 2 == 0 and tok % BLK == 0 else 1
        return jax.shard_map(
            functools.partial(body, cores=cores, chips=seq // 2, heads=heads),
            mesh=split,
            in_specs=(spec, spec, spec, P("head", None), P("head", None, None)),
            out_specs=spec,
            check_vma=False,
        )(queries, keys, values, vertical, slash)

    return run
```

```python
import functools
import math

import jax
import jax.numpy as jnp
from jax import lax
from jax.experimental import pallas as pl
from jax.experimental.pallas import tpu as pltpu
from jax.sharding import Mesh, PartitionSpec as P

BLK = 64
BIG = 1.0e30
LIVE, DEAD, OWN, PICKED = 0, 1, 2, 3
BF16, F32 = jnp.bfloat16, jnp.float32


def arrange_kernel(k_ref, v_ref, o_ref):
    width = v_ref.shape[0]
    head_dim = o_ref.shape[2] - width
    for h in range(o_ref.shape[0]):
        o_ref[h, :, :head_dim] = k_ref[:, h * head_dim : (h + 1) * head_dim]
        o_ref[h, :, head_dim:] = v_ref[:, h * head_dim : (h + 1) * head_dim].T


def arrange(keys, values, heads):
    tok, width = keys.shape
    head_dim = width // heads
    return pl.pallas_call(
        arrange_kernel,
        out_shape=jax.ShapeDtypeStruct((heads, tok, head_dim + tok), BF16),
    )(keys, values)


def step_kernel(code_ref, q_ref, pick_ref, *rest, parts, first, last, span, head_dim, group):
    part_refs, rest = rest[:parts], rest[parts:]
    if not first:
        (acc_in, stat_in, _), rest = rest[:3], rest[3:]
    if last:
        out_ref, rest = rest[0], rest[1:]
    else:
        (acc_out, stat_out, mark_out), rest = rest[:3], rest[3:]
        mark_out[...] = jnp.zeros(mark_out.shape, BF16)
    qext, etile, score_a, score_b = rest
    rows = BLK * group
    chunks, _, wide, _ = part_refs[0].shape
    per_part = chunks * wide // BLK
    slots = parts * per_part
    size = per_part * BLK
    per_q = q_ref.shape[1] // BLK
    blocks_here = q_ref.shape[0] * per_q
    scale = math.log2(math.e) / math.sqrt(head_dim)

    token = lax.rem(lax.broadcasted_iota(jnp.int32, (rows, head_dim), 0), BLK)
    column = lax.broadcasted_iota(jnp.int32, (rows, head_dim), 1)
    masked = ((column < BLK) & (column > token)) | (column == BLK)
    qext[...] = jnp.where(masked, -BIG, 0.0).astype(BF16)
    key_iota = lax.broadcasted_iota(jnp.int32, (BLK, head_dim), 0)
    lane = lax.broadcasted_iota(jnp.int32, (BLK, head_dim), 1)
    etile[LIVE] = jnp.zeros((BLK, head_dim), BF16)
    etile[DEAD] = jnp.where(lane == BLK, 1.0, 0.0).astype(BF16)
    etile[OWN] = jnp.where(lane == key_iota, 1.0, 0.0).astype(BF16)

    def place(here, g):
        start = pl.multiple_of(lax.rem(here, per_q) * BLK, BLK)
        return lax.div(here, per_q), pl.ds(start, BLK), pl.ds(g * head_dim, head_dim)

    def stage(head, ahead, ahead_buffer, here, buffer, top):
        query = jnp.concatenate(
            [q_ref[place(ahead, head * group + g)] for g in range(group)], axis=0
        )
        query = jnp.concatenate([query, qext[...]], axis=1)
        at = head * blocks_here + here if here is not None else None
        if here is not None and not first:
            before = stat_in[at, :8]
            top = jnp.maximum(top, before)
            fade = jnp.exp2((before - top) * scale)
        ahead_top = jnp.full((8, rows), -jnp.inf, F32)
        shares, values = [], []
        for p, part in enumerate(part_refs):
            left = [part[c, head, :, pl.ds(0, head_dim)] for c in range(chunks)]
            right = [
                etile[code_ref[head, ahead, p * per_part + i]] for i in range(per_part)
            ]
            key = jnp.concatenate(
                [jnp.concatenate(left, axis=0), jnp.concatenate(right, axis=0)], axis=1
            )
            tile = lax.dot_general(
                key, query, (((1,), (1,)), ((), ())), preferred_element_type=F32
            )
            ahead_buffer[pl.ds(p * size, size), :] = tile
            ahead_top = jnp.maximum(
                ahead_top, jnp.max(tile.reshape(size // 8, 8, rows), axis=0)
            )
            if here is not None:
                tile = buffer[pl.ds(p * size, size), :].reshape(size // 8, 8, rows)
                expo = jnp.exp2((tile - top[None]) * scale)
                shares.append(expo.reshape(size, rows).astype(BF16))
                values += [part[c, head, :, pl.ds(head_dim, wide)] for c in range(chunks)]
        ahead_top = jnp.broadcast_to(jnp.max(ahead_top, axis=0, keepdims=True), (8, rows))
        if here is None:
            return ahead_top
        value = jnp.concatenate(values, axis=1)
        value = jnp.concatenate([value, jnp.ones((16, value.shape[1]), BF16)], axis=0)
        both = jnp.dot(value, jnp.concatenate(shares, axis=0), preferred_element_type=F32)
        mixed, weight = both[:head_dim], both[head_dim : head_dim + 8]
        if not first:
            mixed = mixed + acc_in[at] * fade[:1]
            weight = weight + stat_in[at, 8:] * fade
        if not last:
            acc_out[at] = mixed
            stat_out[at, :8] = top
            stat_out[at, 8:] = weight
            return ahead_top
        result = (mixed / weight[:1]).T.astype(BF16)
        for g in range(group):
            out_ref[place(here, (head - span[0]) * group + g)] = result[g * BLK : (g + 1) * BLK]
        return ahead_top

    for head in range(*span):
        for slot in range(slots):
            etile[PICKED + slot] = pick_ref[head, slot]

        def two(step, top):
            top = stage(head, 2 * step + 1, score_b, 2 * step, score_a, top)
            ahead = jnp.minimum(2 * step + 2, blocks_here - 1)
            return stage(head, ahead, score_a, 2 * step + 1, score_b, top)

        top = stage(head, 0, score_a, None, None, None)
        lax.fori_loop(0, blocks_here // 2, two, top)


def attend_step(code, query, pick, parts, state, span, last, head_dim, group):
    heads, slots = pick.shape[:2]
    blocks_here = query.shape[0] * query.shape[1] // BLK
    rows = BLK * group
    smem = pl.BlockSpec(memory_space=pltpu.SMEM)
    vmem = pl.BlockSpec(memory_space=pltpu.VMEM)
    carried = (
        jax.ShapeDtypeStruct((heads * blocks_here, head_dim, rows), F32),
        jax.ShapeDtypeStruct((heads * blocks_here, 16, rows), F32),
        jax.ShapeDtypeStruct((16, 128), BF16),
    )
    count = span[1] - span[0]
    out = jax.ShapeDtypeStruct(query.shape[:2] + (count * group * head_dim,), BF16)
    first = state is None
    state = () if first else tuple(state)
    work = count * blocks_here * rows * slots * BLK
    return pl.pallas_call(
        functools.partial(
            step_kernel,
            parts=len(parts),
            first=first,
            last=last,
            span=span,
            head_dim=head_dim,
            group=group,
        ),
        out_shape=out if last else carried,
        in_specs=[smem] + [vmem] * (2 + len(parts) + len(state)),
        out_specs=vmem if last else (vmem,) * 3,
        scratch_shapes=[
            pltpu.VMEM((rows, head_dim), BF16),
            pltpu.VMEM((PICKED + slots, BLK, head_dim), BF16),
            pltpu.VMEM((slots * BLK, rows), F32),
            pltpu.VMEM((slots * BLK, rows), F32),
        ],
        compiler_params=pltpu.CompilerParams(vmem_limit_bytes=16 << 20),
        cost_estimate=pl.CostEstimate(
            flops=4 * work * head_dim, transcendentals=work, bytes_accessed=8 << 20
        ),
    )(code, query, pick, *parts, *state)


def body(queries, keys, values, vertical, slash, *, cores, chips, heads):
    tok, q_width = queries.shape
    all_heads = vertical.shape[0] * heads
    head_dim = keys.shape[1] // all_heads
    group = q_width // keys.shape[1]
    ways = cores * heads
    mine = all_heads // ways
    axes = ("head", "core") if cores > 1 else ("head",)
    groups = chips if cores > 1 else chips * 2
    per_group = tok * ways // BLK
    chip = lax.axis_index("chip")
    if cores == 1:
        chip = chip * 2 + lax.axis_index("core")
    relative = cores > 1 and chips == 8
    swap = functools.partial(
        lax.all_to_all, axis_name=axes, split_axis=0, concat_axis=0, tiled=True
    )

    if relative:
        pair = swap(arrange(keys, values, all_heads).reshape(ways, mine, tok, head_dim + tok))
    else:
        pair = jnp.concatenate(
            [keys.reshape(tok, ways, mine, head_dim), values.reshape(tok, ways, mine, head_dim)],
            axis=3,
        )
        pair = swap(pair.transpose(1, 2, 0, 3))
    query = queries.reshape(tok, ways, q_width // ways).transpose(1, 0, 2)

    pair, vertical, slash = lax.optimization_barrier((pair, vertical, slash))

    along = tok // BLK
    local = jnp.arange(per_group, dtype=jnp.int32)
    if cores > 1:
        local = local.reshape(cores, heads, along).swapaxes(0, 1).reshape(-1)
    first_head = lax.axis_index("core") * mine if cores > 1 else 0
    slash = lax.dynamic_slice_in_dim(slash, first_head, mine, axis=0)
    vertical = lax.dynamic_slice_in_dim(vertical, first_head, mine, axis=0)
    lists = lax.dynamic_slice_in_dim(slash, chip * per_group, per_group, axis=1)
    if cores > 1:
        lists = (
            lists.reshape(mine, cores, heads, along, -1).swapaxes(1, 2).reshape(lists.shape)
        )
    ids = chip * per_group + local

    def masks(source):
        nat = (source[:, None] * per_group + local).reshape(-1)
        listed = jnp.any(lists[:, :, :, None] == nat, axis=2)
        slot = PICKED + jnp.arange(nat.shape[0], dtype=jnp.int32)
        code = jnp.where(
            listed,
            LIVE,
            jnp.where(nat == ids[:, None], OWN, jnp.where(nat > ids[:, None], DEAD, slot)),
        )
        position = nat[:, None] * BLK + jnp.arange(BLK, dtype=jnp.int32)
        hidden = jnp.all(vertical[:, None, None, :] != position[..., None], axis=3)
        lane = jnp.arange(head_dim, dtype=jnp.int32) == BLK
        return code, (hidden[..., None] & lane).astype(BF16)

    def attend(query, table, parts, state, last):
        state = None if state is None else tuple(state)
        run = functools.partial(attend_step, table[0], query, table[1], parts, state)
        if not last:
            return run((0, mine), False, head_dim, group)
        return run((0, mine), True, head_dim, group)

    state = None
    if relative:
        across = [(i, i ^ 1) for i in range(chips)]
        up = [(i, i + 2) for i in range(chips - 2)]
        final = chips // 2 - 1
        col = jnp.stack([chip % 2, 1 - chip % 2])
        tables = []
        for n in range(final + 1):
            row = chip // 2 - n
            tables.append(masks(jnp.where(row < 0, groups, 2 * row + col)))
        code, query = lax.optimization_barrier((tables[0][0], query))
        tables[0] = (code, tables[0][1])
        query = swap(query).reshape(-1, max(tok, BLK), q_width // ways)
        part, waiting = pair, None
        for n in range(final + 2):
            fetched = None
            if n <= final:
                if n == 1:
                    part, tables = lax.optimization_barrier((part, tables))
                if state is not None:
                    part, mark = lax.optimization_barrier((part, state[2]))
                    state = state[:2] + (mark,)
                fetched = (part, lax.ppermute(part, "chip", across))
                part = lax.ppermute(part, "chip", up) if n < final else None
            if n:
                state = attend(query, tables[n - 1], waiting, state, n > final)
            waiting = fetched
    else:
        query = swap(query).reshape(-1, max(tok, BLK), q_width // ways)
        axis = "chip" if cores > 1 else ("chip", "core")
        rows = pair.transpose(1, 0, 2, 3).reshape(mine, -1, 2 * head_dim)
        rows = lax.all_gather(rows, axis, axis=1, tiled=True)
        pieces = rows.shape[1] // (2 * BLK)
        turned = rows[..., head_dim:].reshape(mine, pieces, 2 * BLK, head_dim).swapaxes(2, 3)
        rows = rows[..., :head_dim].reshape(mine, pieces, 2 * BLK, head_dim)
        rows = jnp.concatenate([rows, turned], axis=3).swapaxes(0, 1)
        each = per_group // 2
        order = (chip + jnp.arange(groups, dtype=jnp.int32)) % groups
        rows = jnp.roll(rows.reshape((groups, each) + rows.shape[1:]), -chip, axis=0)
        many = math.gcd(groups, 4)
        for g in range(0, groups, many):
            part = rows[g : g + many].reshape((many * each,) + rows.shape[2:])
            state = attend(query, masks(order[g : g + many]), (part,), state, g + many == groups)

    out = swap(state.reshape(ways, tok, q_width // ways))
    return out.transpose(1, 0, 2).reshape(tok, q_width)


def solution(mesh):
    seq, heads = mesh.shape["seq"], mesh.shape["head"]
    split = Mesh(mesh.devices.reshape(seq // 2, 2, heads), ("chip", "core", "head"))
    spec = P(("chip", "core", "head"), None)

    def run(queries, keys, values, vertical, slash):
        local_heads = vertical.shape[0] // heads
        tok = queries.shape[0] // (seq * heads)
        cores = 2 if local_heads % 2 == 0 and tok % BLK == 0 else 1
        return jax.shard_map(
            functools.partial(body, cores=cores, chips=seq // 2, heads=heads),
            mesh=split,
            in_specs=(spec, spec, spec, P("head", None), P("head", None, None)),
            out_specs=spec,
            check_vma=False,
        )(queries, keys, values, vertical, slash)

    return run
```

```python
import functools
import math

import jax
import jax.numpy as jnp
from jax import lax
from jax.experimental import pallas as pl
from jax.experimental.pallas import tpu as pltpu
from jax.sharding import Mesh, PartitionSpec as P

BLK = 64
BIG = 1.0e30
LIVE, DEAD, OWN, PICKED = 0, 1, 2, 3
BF16, F32 = jnp.bfloat16, jnp.float32


def arrange_kernel(k_ref, v_ref, o_ref):
    width = v_ref.shape[0]
    head_dim = o_ref.shape[2] - width
    for h in range(o_ref.shape[0]):
        o_ref[h, :, :head_dim] = k_ref[:, h * head_dim : (h + 1) * head_dim]
        o_ref[h, :, head_dim:] = v_ref[:, h * head_dim : (h + 1) * head_dim].T


def arrange(keys, values, heads):
    tok, width = keys.shape
    head_dim = width // heads
    return pl.pallas_call(
        arrange_kernel,
        out_shape=jax.ShapeDtypeStruct((heads, tok, head_dim + tok), BF16),
    )(keys, values)


def step_kernel(code_ref, q_ref, pick_ref, *rest, parts, first, last, span, head_dim, group):
    part_refs = []
    for count in parts:
        part_refs.append(rest[:count])
        rest = rest[count:]
    if not first:
        (acc_in, stat_in, _), rest = rest[:3], rest[3:]
    if last:
        out_ref, rest = rest[0], rest[1:]
    else:
        (acc_out, stat_out, mark_out), rest = rest[:3], rest[3:]
        mark_out[...] = jnp.zeros(mark_out.shape, BF16)
    qext, etile, score_a, score_b = rest
    rows = BLK * group
    chunks, _, wide, _ = part_refs[0][0].shape
    per_part = chunks * wide // BLK
    slots = len(parts) * per_part
    size = per_part * BLK
    per_q = q_ref.shape[1] // BLK
    blocks_here = q_ref.shape[0] * per_q
    scale = math.log2(math.e) / math.sqrt(head_dim)

    token = lax.rem(lax.broadcasted_iota(jnp.int32, (rows, head_dim), 0), BLK)
    column = lax.broadcasted_iota(jnp.int32, (rows, head_dim), 1)
    masked = ((column < BLK) & (column > token)) | (column == BLK)
    qext[...] = jnp.where(masked, -BIG, 0.0).astype(BF16)
    key_iota = lax.broadcasted_iota(jnp.int32, (BLK, head_dim), 0)
    lane = lax.broadcasted_iota(jnp.int32, (BLK, head_dim), 1)
    etile[LIVE] = jnp.zeros((BLK, head_dim), BF16)
    etile[DEAD] = jnp.where(lane == BLK, 1.0, 0.0).astype(BF16)
    etile[OWN] = jnp.where(lane == key_iota, 1.0, 0.0).astype(BF16)

    def held(p, head, c):
        for ref in part_refs[p]:
            if head < ref.shape[1]:
                return ref.at[c, head]
            head -= ref.shape[1]

    def place(here, g):
        start = pl.multiple_of(lax.rem(here, per_q) * BLK, BLK)
        return lax.div(here, per_q), pl.ds(start, BLK), pl.ds(g * head_dim, head_dim)

    def stage(head, ahead, ahead_buffer, here, buffer, top):
        query = jnp.concatenate(
            [q_ref[place(ahead, head * group + g)] for g in range(group)], axis=0
        )
        query = jnp.concatenate([query, qext[...]], axis=1)
        at = head * blocks_here + here if here is not None else None
        if here is not None and not first:
            before = stat_in[at, :8]
            top = jnp.maximum(top, before)
            fade = jnp.exp2((before - top) * scale)
        ahead_top = jnp.full((8, rows), -jnp.inf, F32)
        shares, values = [], []
        for p in range(len(parts)):
            left = [held(p, head, c)[:, pl.ds(0, head_dim)] for c in range(chunks)]
            right = [
                etile[code_ref[head, ahead, p * per_part + i]] for i in range(per_part)
            ]
            key = jnp.concatenate(
                [jnp.concatenate(left, axis=0), jnp.concatenate(right, axis=0)], axis=1
            )
            tile = lax.dot_general(
                key, query, (((1,), (1,)), ((), ())), preferred_element_type=F32
            )
            ahead_buffer[pl.ds(p * size, size), :] = tile
            ahead_top = jnp.maximum(
                ahead_top, jnp.max(tile.reshape(size // 8, 8, rows), axis=0)
            )
            if here is not None:
                tile = buffer[pl.ds(p * size, size), :].reshape(size // 8, 8, rows)
                expo = jnp.exp2((tile - top[None]) * scale)
                shares.append(expo.reshape(size, rows).astype(BF16))
                values += [held(p, head, c)[:, pl.ds(head_dim, wide)] for c in range(chunks)]
        ahead_top = jnp.broadcast_to(jnp.max(ahead_top, axis=0, keepdims=True), (8, rows))
        if here is None:
            return ahead_top
        value = jnp.concatenate(values, axis=1)
        value = jnp.concatenate([value, jnp.ones((16, value.shape[1]), BF16)], axis=0)
        both = jnp.dot(value, jnp.concatenate(shares, axis=0), preferred_element_type=F32)
        mixed, weight = both[:head_dim], both[head_dim : head_dim + 8]
        if not first:
            mixed = mixed + acc_in[at] * fade[:1]
            weight = weight + stat_in[at, 8:] * fade
        if not last:
            acc_out[at] = mixed
            stat_out[at, :8] = top
            stat_out[at, 8:] = weight
            return ahead_top
        result = (mixed / weight[:1]).T.astype(BF16)
        for g in range(group):
            out_ref[place(here, (head - span[0]) * group + g)] = result[g * BLK : (g + 1) * BLK]
        return ahead_top

    for head in range(*span):
        for slot in range(slots):
            etile[PICKED + slot] = pick_ref[head, slot]

        def two(step, top):
            top = stage(head, 2 * step + 1, score_b, 2 * step, score_a, top)
            ahead = jnp.minimum(2 * step + 2, blocks_here - 1)
            return stage(head, ahead, score_a, 2 * step + 1, score_b, top)

        top = stage(head, 0, score_a, None, None, None)
        lax.fori_loop(0, blocks_here // 2, two, top)


def attend_step(code, query, pick, parts, state, span, last, head_dim, group):
    heads, slots = pick.shape[:2]
    blocks_here = query.shape[0] * query.shape[1] // BLK
    rows = BLK * group
    smem = pl.BlockSpec(memory_space=pltpu.SMEM)
    vmem = pl.BlockSpec(memory_space=pltpu.VMEM)
    carried = (
        jax.ShapeDtypeStruct((heads * blocks_here, head_dim, rows), F32),
        jax.ShapeDtypeStruct((heads * blocks_here, 16, rows), F32),
        jax.ShapeDtypeStruct((16, 128), BF16),
    )
    count = span[1] - span[0]
    out = jax.ShapeDtypeStruct(query.shape[:2] + (count * group * head_dim,), BF16)
    arrays = [x for part in parts for x in part]
    first = state is None
    state = () if first else tuple(state)
    work = count * blocks_here * rows * slots * BLK
    return pl.pallas_call(
        functools.partial(
            step_kernel,
            parts=tuple(len(part) for part in parts),
            first=first,
            last=last,
            span=span,
            head_dim=head_dim,
            group=group,
        ),
        out_shape=out if last else carried,
        in_specs=[smem] + [vmem] * (2 + len(arrays) + len(state)),
        out_specs=vmem if last else (vmem,) * 3,
        scratch_shapes=[
            pltpu.VMEM((rows, head_dim), BF16),
            pltpu.VMEM((PICKED + slots, BLK, head_dim), BF16),
            pltpu.VMEM((slots * BLK, rows), F32),
            pltpu.VMEM((slots * BLK, rows), F32),
        ],
        compiler_params=pltpu.CompilerParams(vmem_limit_bytes=16 << 20),
        cost_estimate=pl.CostEstimate(
            flops=4 * work * head_dim, transcendentals=work, bytes_accessed=8 << 20
        ),
    )(code, query, pick, *arrays, *state)


def body(queries, keys, values, vertical, slash, *, cores, chips, heads):
    tok, q_width = queries.shape
    all_heads = vertical.shape[0] * heads
    head_dim = keys.shape[1] // all_heads
    group = q_width // keys.shape[1]
    ways = cores * heads
    mine = all_heads // ways
    axes = ("head", "core") if cores > 1 else ("head",)
    groups = chips if cores > 1 else chips * 2
    per_group = tok * ways // BLK
    chip = lax.axis_index("chip")
    if cores == 1:
        chip = chip * 2 + lax.axis_index("core")
    relative = cores > 1 and chips == 8
    swap = functools.partial(
        lax.all_to_all, axis_name=axes, split_axis=0, concat_axis=0, tiled=True
    )

    if relative:
        pair = swap(arrange(keys, values, all_heads).reshape(ways, mine, tok, head_dim + tok))
    else:
        pair = jnp.concatenate(
            [keys.reshape(tok, ways, mine, head_dim), values.reshape(tok, ways, mine, head_dim)],
            axis=3,
        )
        pair = swap(pair.transpose(1, 2, 0, 3))
    query = queries.reshape(tok, ways, q_width // ways).transpose(1, 0, 2)

    pair, vertical, slash = lax.optimization_barrier((pair, vertical, slash))

    along = tok // BLK
    local = jnp.arange(per_group, dtype=jnp.int32)
    if cores > 1:
        local = local.reshape(cores, heads, along).swapaxes(0, 1).reshape(-1)
    first_head = lax.axis_index("core") * mine if cores > 1 else 0
    slash = lax.dynamic_slice_in_dim(slash, first_head, mine, axis=0)
    vertical = lax.dynamic_slice_in_dim(vertical, first_head, mine, axis=0)
    lists = lax.dynamic_slice_in_dim(slash, chip * per_group, per_group, axis=1)
    if cores > 1:
        lists = (
            lists.reshape(mine, cores, heads, along, -1).swapaxes(1, 2).reshape(lists.shape)
        )
    ids = chip * per_group + local

    def masks(source):
        nat = (source[:, None] * per_group + local).reshape(-1)
        listed = jnp.any(lists[:, :, :, None] == nat, axis=2)
        slot = PICKED + jnp.arange(nat.shape[0], dtype=jnp.int32)
        code = jnp.where(
            listed,
            LIVE,
            jnp.where(nat == ids[:, None], OWN, jnp.where(nat > ids[:, None], DEAD, slot)),
        )
        position = nat[:, None] * BLK + jnp.arange(BLK, dtype=jnp.int32)
        hidden = jnp.all(vertical[:, None, None, :] != position[..., None], axis=3)
        lane = jnp.arange(head_dim, dtype=jnp.int32) == BLK
        return code, (hidden[..., None] & lane).astype(BF16)

    def attend(query, table, parts, state, last):
        state = None if state is None else tuple(state)
        run = functools.partial(attend_step, table[0], query, table[1], parts, state)
        if not last:
            return run((0, mine), False, head_dim, group)
        return run((0, mine), True, head_dim, group)

    state = None
    if relative:
        across = [(i, i ^ 1) for i in range(chips)]
        up = [(i, i + 2) for i in range(chips - 2)]
        final = chips // 2 - 1
        col = jnp.stack([chip % 2, 1 - chip % 2])
        tables = []
        for n in range(final + 1):
            row = chip // 2 - n
            tables.append(masks(jnp.where(row < 0, groups, 2 * row + col)))
        code, query = lax.optimization_barrier((tables[0][0], query))
        tables[0] = (code, tables[0][1])
        query = swap(query).reshape(-1, max(tok, BLK), q_width // ways)
        part, waiting = pair, None
        for n in range(final + 2):
            fetched = None
            if n <= final:
                if n == 1:
                    part, tables = lax.optimization_barrier((part, tables))
                if state is not None:
                    part, mark = lax.optimization_barrier((part, state[2]))
                    state = state[:2] + (mark,)
                if n < final or mine == 1:
                    other = (lax.ppermute(part, "chip", across),)
                else:
                    cut = (mine + 1) // 2
                    other = (
                        lax.ppermute(part[:, :cut], "chip", across),
                        lax.ppermute(waiting[1][0][:, cut:], "chip", up),
                    )
                fetched = ((part,), other)
                part = lax.ppermute(part, "chip", up) if n < final else None
            if n:
                state = attend(query, tables[n - 1], waiting, state, n > final)
            waiting = fetched
    else:
        query = swap(query).reshape(-1, max(tok, BLK), q_width // ways)
        axis = "chip" if cores > 1 else ("chip", "core")
        rows = pair.transpose(1, 0, 2, 3).reshape(mine, -1, 2 * head_dim)
        rows = lax.all_gather(rows, axis, axis=1, tiled=True)
        pieces = rows.shape[1] // (2 * BLK)
        turned = rows[..., head_dim:].reshape(mine, pieces, 2 * BLK, head_dim).swapaxes(2, 3)
        rows = rows[..., :head_dim].reshape(mine, pieces, 2 * BLK, head_dim)
        rows = jnp.concatenate([rows, turned], axis=3).swapaxes(0, 1)
        each = per_group // 2
        order = (chip + jnp.arange(groups, dtype=jnp.int32)) % groups
        rows = jnp.roll(rows.reshape((groups, each) + rows.shape[1:]), -chip, axis=0)
        many = math.gcd(groups, 4)
        for g in range(0, groups, many):
            part = rows[g : g + many].reshape((many * each,) + rows.shape[2:])
            state = attend(query, masks(order[g : g + many]), ((part,),), state, g + many == groups)

    out = swap(state.reshape(ways, tok, q_width // ways))
    return out.transpose(1, 0, 2).reshape(tok, q_width)


def solution(mesh):
    seq, heads = mesh.shape["seq"], mesh.shape["head"]
    split = Mesh(mesh.devices.reshape(seq // 2, 2, heads), ("chip", "core", "head"))
    spec = P(("chip", "core", "head"), None)

    def run(queries, keys, values, vertical, slash):
        local_heads = vertical.shape[0] // heads
        tok = queries.shape[0] // (seq * heads)
        cores = 2 if local_heads % 2 == 0 and tok % BLK == 0 else 1
        return jax.shard_map(
            functools.partial(body, cores=cores, chips=seq // 2, heads=heads),
            mesh=split,
            in_specs=(spec, spec, spec, P("head", None), P("head", None, None)),
            out_specs=spec,
            check_vma=False,
        )(queries, keys, values, vertical, slash)

    return run
```

```python
import functools
import math

import jax
import jax.numpy as jnp
from jax import lax
from jax.experimental import pallas as pl
from jax.experimental.pallas import tpu as pltpu
from jax.sharding import Mesh, PartitionSpec as P

BLK = 64
BIG = 1.0e30
LIVE, DEAD, OWN, PICKED = 0, 1, 2, 3
BF16, F32 = jnp.bfloat16, jnp.float32


def arrange_kernel(me_ref, k_ref, v_ref, *o_refs):
    mine, width, _ = o_refs[0].shape
    head_dim = o_refs[0].shape[2] - width
    for m, o_ref in enumerate(o_refs):
        device = lax.bitwise_xor(me_ref[0], m)
        first = (lax.rem(device, 2) * 2 + lax.div(device, 2)) * mine
        for h in range(mine):
            columns = pl.ds(pl.multiple_of((first + h) * head_dim, head_dim), head_dim)
            o_ref[h, :, :head_dim] = k_ref[:, columns]
            o_ref[h, :, head_dim:] = v_ref[:, columns].T


def arrange(me, keys, values, mine, head_dim):
    tok = keys.shape[0]
    vmem = pl.BlockSpec(memory_space=pltpu.VMEM)
    return pl.pallas_call(
        arrange_kernel,
        out_shape=[jax.ShapeDtypeStruct((mine, tok, head_dim + tok), BF16)] * 4,
        in_specs=[pl.BlockSpec(memory_space=pltpu.SMEM), vmem, vmem],
        out_specs=[vmem] * 4,
    )(me, keys, values)


def step_kernel(code_ref, q_ref, pick_ref, *rest, parts, first, last, span, head_dim, group):
    part_refs = []
    for count in parts:
        part_refs.append(rest[:count])
        rest = rest[count:]
    if not first:
        (acc_in, stat_in, _), rest = rest[:3], rest[3:]
    if last:
        out_ref, rest = rest[0], rest[1:]
    else:
        (acc_out, stat_out, mark_out), rest = rest[:3], rest[3:]
        mark_out[...] = jnp.zeros(mark_out.shape, BF16)
    qext, etile, score_a, score_b = rest
    rows = BLK * group
    chunks, _, wide, _ = part_refs[0][0].shape
    per_part = chunks * wide // BLK
    slots = len(parts) * per_part
    size = per_part * BLK
    per_q = q_ref.shape[1] // BLK
    blocks_here = q_ref.shape[0] * per_q
    scale = math.log2(math.e) / math.sqrt(head_dim)

    token = lax.rem(lax.broadcasted_iota(jnp.int32, (rows, head_dim), 0), BLK)
    column = lax.broadcasted_iota(jnp.int32, (rows, head_dim), 1)
    masked = ((column < BLK) & (column > token)) | (column == BLK)
    qext[...] = jnp.where(masked, -BIG, 0.0).astype(BF16)
    key_iota = lax.broadcasted_iota(jnp.int32, (BLK, head_dim), 0)
    lane = lax.broadcasted_iota(jnp.int32, (BLK, head_dim), 1)
    etile[LIVE] = jnp.zeros((BLK, head_dim), BF16)
    etile[DEAD] = jnp.where(lane == BLK, 1.0, 0.0).astype(BF16)
    etile[OWN] = jnp.where(lane == key_iota, 1.0, 0.0).astype(BF16)

    def held(p, head, c):
        for ref in part_refs[p]:
            if head < ref.shape[1]:
                return ref.at[c, head]
            head -= ref.shape[1]

    def place(here, g):
        start = pl.multiple_of(lax.rem(here, per_q) * BLK, BLK)
        return lax.div(here, per_q), pl.ds(start, BLK), pl.ds(g * head_dim, head_dim)

    def stage(head, ahead, ahead_buffer, here, buffer, top):
        query = jnp.concatenate(
            [q_ref[place(ahead, head * group + g)] for g in range(group)], axis=0
        )
        query = jnp.concatenate([query, qext[...]], axis=1)
        at = head * blocks_here + here if here is not None else None
        if here is not None and not first:
            before = stat_in[at, :8]
            top = jnp.maximum(top, before)
            fade = jnp.exp2((before - top) * scale)
        ahead_top = jnp.full((8, rows), -jnp.inf, F32)
        shares, values = [], []
        for p in range(len(parts)):
            left = [held(p, head, c)[:, pl.ds(0, head_dim)] for c in range(chunks)]
            right = [
                etile[code_ref[head, ahead, p * per_part + i]] for i in range(per_part)
            ]
            key = jnp.concatenate(
                [jnp.concatenate(left, axis=0), jnp.concatenate(right, axis=0)], axis=1
            )
            tile = lax.dot_general(
                key, query, (((1,), (1,)), ((), ())), preferred_element_type=F32
            )
            ahead_buffer[pl.ds(p * size, size), :] = tile
            ahead_top = jnp.maximum(
                ahead_top, jnp.max(tile.reshape(size // 8, 8, rows), axis=0)
            )
            if here is not None:
                tile = buffer[pl.ds(p * size, size), :].reshape(size // 8, 8, rows)
                expo = jnp.exp2((tile - top[None]) * scale)
                shares.append(expo.reshape(size, rows).astype(BF16))
                values += [held(p, head, c)[:, pl.ds(head_dim, wide)] for c in range(chunks)]
        ahead_top = jnp.broadcast_to(jnp.max(ahead_top, axis=0, keepdims=True), (8, rows))
        if here is None:
            return ahead_top
        value = jnp.concatenate(values, axis=1)
        value = jnp.concatenate([value, jnp.ones((16, value.shape[1]), BF16)], axis=0)
        both = jnp.dot(value, jnp.concatenate(shares, axis=0), preferred_element_type=F32)
        mixed, weight = both[:head_dim], both[head_dim : head_dim + 8]
        if not first:
            mixed = mixed + acc_in[at] * fade[:1]
            weight = weight + stat_in[at, 8:] * fade
        if not last:
            acc_out[at] = mixed
            stat_out[at, :8] = top
            stat_out[at, 8:] = weight
            return ahead_top
        result = (mixed / weight[:1]).T.astype(BF16)
        for g in range(group):
            out_ref[place(here, (head - span[0]) * group + g)] = result[g * BLK : (g + 1) * BLK]
        return ahead_top

    for head in range(*span):
        for slot in range(slots):
            etile[PICKED + slot] = pick_ref[head, slot]

        def two(step, top):
            top = stage(head, 2 * step + 1, score_b, 2 * step, score_a, top)
            ahead = jnp.minimum(2 * step + 2, blocks_here - 1)
            return stage(head, ahead, score_a, 2 * step + 1, score_b, top)

        top = stage(head, 0, score_a, None, None, None)
        lax.fori_loop(0, blocks_here // 2, two, top)


def attend_step(code, query, pick, parts, state, span, last, head_dim, group):
    heads, slots = pick.shape[:2]
    blocks_here = query.shape[0] * query.shape[1] // BLK
    rows = BLK * group
    smem = pl.BlockSpec(memory_space=pltpu.SMEM)
    vmem = pl.BlockSpec(memory_space=pltpu.VMEM)
    carried = (
        jax.ShapeDtypeStruct((heads * blocks_here, head_dim, rows), F32),
        jax.ShapeDtypeStruct((heads * blocks_here, 16, rows), F32),
        jax.ShapeDtypeStruct((16, 128), BF16),
    )
    count = span[1] - span[0]
    out = jax.ShapeDtypeStruct(query.shape[:2] + (count * group * head_dim,), BF16)
    arrays = [x for part in parts for x in part]
    first = state is None
    state = () if first else tuple(state)
    work = count * blocks_here * rows * slots * BLK
    return pl.pallas_call(
        functools.partial(
            step_kernel,
            parts=tuple(len(part) for part in parts),
            first=first,
            last=last,
            span=span,
            head_dim=head_dim,
            group=group,
        ),
        out_shape=out if last else carried,
        in_specs=[smem] + [vmem] * (2 + len(arrays) + len(state)),
        out_specs=vmem if last else (vmem,) * 3,
        scratch_shapes=[
            pltpu.VMEM((rows, head_dim), BF16),
            pltpu.VMEM((PICKED + slots, BLK, head_dim), BF16),
            pltpu.VMEM((slots * BLK, rows), F32),
            pltpu.VMEM((slots * BLK, rows), F32),
        ],
        compiler_params=pltpu.CompilerParams(vmem_limit_bytes=16 << 20),
        cost_estimate=pl.CostEstimate(
            flops=4 * work * head_dim, transcendentals=work, bytes_accessed=8 << 20
        ),
    )(code, query, pick, *arrays, *state)


def body(queries, keys, values, vertical, slash, *, cores, chips, heads):
    tok, q_width = queries.shape
    all_heads = vertical.shape[0] * heads
    head_dim = keys.shape[1] // all_heads
    group = q_width // keys.shape[1]
    ways = cores * heads
    mine = all_heads // ways
    axes = ("head", "core") if cores > 1 else ("head",)
    groups = chips if cores > 1 else chips * 2
    per_group = tok * ways // BLK
    chip = lax.axis_index("chip")
    if cores == 1:
        chip = chip * 2 + lax.axis_index("core")
    relative = cores > 1 and chips == 8 and heads == 2
    swap = functools.partial(
        lax.all_to_all, axis_name=axes, split_axis=0, concat_axis=0, tiled=True
    )

    if relative:
        me = lax.axis_index("core") * 2 + lax.axis_index("head")
        pieces = arrange(me[None].astype(jnp.int32), keys, values, mine, head_dim)
        pair = [pieces[0]] + [
            lax.ppermute(pieces[m], ("core", "head"), [(i, i ^ m) for i in range(4)])
            for m in (1, 3, 2)
        ]
        pair = jnp.stack([pair[0], pair[1], pair[3], pair[2]])
    else:
        pair = jnp.concatenate(
            [keys.reshape(tok, ways, mine, head_dim), values.reshape(tok, ways, mine, head_dim)],
            axis=3,
        )
        pair = swap(pair.transpose(1, 2, 0, 3))
    query = queries.reshape(tok, ways, q_width // ways).transpose(1, 0, 2)

    pair, vertical, slash = lax.optimization_barrier((pair, vertical, slash))

    along = tok // BLK
    local = jnp.arange(per_group, dtype=jnp.int32)
    if cores > 1:
        local = local.reshape(cores, heads, along).swapaxes(0, 1).reshape(-1)
    local_keys = local
    if relative:
        order = jnp.stack([me ^ m for m in range(4)]).astype(jnp.int32)
        local_keys = (order[:, None] * along + jnp.arange(along, dtype=jnp.int32)).reshape(-1)
    first_head = lax.axis_index("core") * mine if cores > 1 else 0
    slash = lax.dynamic_slice_in_dim(slash, first_head, mine, axis=0)
    vertical = lax.dynamic_slice_in_dim(vertical, first_head, mine, axis=0)
    lists = lax.dynamic_slice_in_dim(slash, chip * per_group, per_group, axis=1)
    if cores > 1:
        lists = (
            lists.reshape(mine, cores, heads, along, -1).swapaxes(1, 2).reshape(lists.shape)
        )
    ids = chip * per_group + local

    def masks(source):
        nat = (source[:, None] * per_group + local_keys).reshape(-1)
        listed = jnp.any(lists[:, :, :, None] == nat, axis=2)
        slot = PICKED + jnp.arange(nat.shape[0], dtype=jnp.int32)
        code = jnp.where(
            listed,
            LIVE,
            jnp.where(nat == ids[:, None], OWN, jnp.where(nat > ids[:, None], DEAD, slot)),
        )
        position = nat[:, None] * BLK + jnp.arange(BLK, dtype=jnp.int32)
        hidden = jnp.all(vertical[:, None, None, :] != position[..., None], axis=3)
        lane = jnp.arange(head_dim, dtype=jnp.int32) == BLK
        return code, (hidden[..., None] & lane).astype(BF16)

    def attend(query, table, parts, state, last):
        state = None if state is None else tuple(state)
        run = functools.partial(attend_step, table[0], query, table[1], parts, state)
        if not last:
            return run((0, mine), False, head_dim, group)
        return run((0, mine), True, head_dim, group)

    state = None
    if relative:
        across = [(i, i ^ 1) for i in range(chips)]
        up = [(i, i + 2) for i in range(chips - 2)]
        final = chips // 2 - 1
        col = jnp.stack([chip % 2, 1 - chip % 2])
        tables = []
        for n in range(final + 1):
            row = chip // 2 - n
            tables.append(masks(jnp.where(row < 0, groups, 2 * row + col)))
        code, query = lax.optimization_barrier((tables[0][0], query))
        tables[0] = (code, tables[0][1])
        query = swap(query).reshape(-1, max(tok, BLK), q_width // ways)
        part, waiting = pair, None
        for n in range(final + 2):
            fetched = None
            if n <= final:
                if n == 1:
                    part, tables = lax.optimization_barrier((part, tables))
                if state is not None:
                    part, mark = lax.optimization_barrier((part, state[2]))
                    state = state[:2] + (mark,)
                if n < final or mine == 1:
                    other = (lax.ppermute(part, "chip", across),)
                else:
                    cut = (mine + 1) // 2
                    other = (
                        lax.ppermute(part[:, :cut], "chip", across),
                        lax.ppermute(waiting[1][0][:, cut:], "chip", up),
                    )
                fetched = ((part,), other)
                part = lax.ppermute(part, "chip", up) if n < final else None
            if n:
                state = attend(query, tables[n - 1], waiting, state, n > final)
            waiting = fetched
    else:
        query = swap(query).reshape(-1, max(tok, BLK), q_width // ways)
        axis = "chip" if cores > 1 else ("chip", "core")
        rows = pair.transpose(1, 0, 2, 3).reshape(mine, -1, 2 * head_dim)
        rows = lax.all_gather(rows, axis, axis=1, tiled=True)
        pieces = rows.shape[1] // (2 * BLK)
        turned = rows[..., head_dim:].reshape(mine, pieces, 2 * BLK, head_dim).swapaxes(2, 3)
        rows = rows[..., :head_dim].reshape(mine, pieces, 2 * BLK, head_dim)
        rows = jnp.concatenate([rows, turned], axis=3).swapaxes(0, 1)
        each = per_group // 2
        order = (chip + jnp.arange(groups, dtype=jnp.int32)) % groups
        rows = jnp.roll(rows.reshape((groups, each) + rows.shape[1:]), -chip, axis=0)
        many = math.gcd(groups, 4)
        for g in range(0, groups, many):
            part = rows[g : g + many].reshape((many * each,) + rows.shape[2:])
            state = attend(query, masks(order[g : g + many]), ((part,),), state, g + many == groups)

    out = swap(state.reshape(ways, tok, q_width // ways))
    return out.transpose(1, 0, 2).reshape(tok, q_width)


def solution(mesh):
    seq, heads = mesh.shape["seq"], mesh.shape["head"]
    split = Mesh(mesh.devices.reshape(seq // 2, 2, heads), ("chip", "core", "head"))
    spec = P(("chip", "core", "head"), None)

    def run(queries, keys, values, vertical, slash):
        local_heads = vertical.shape[0] // heads
        tok = queries.shape[0] // (seq * heads)
        cores = 2 if local_heads % 2 == 0 and tok % BLK == 0 else 1
        return jax.shard_map(
            functools.partial(body, cores=cores, chips=seq // 2, heads=heads),
            mesh=split,
            in_specs=(spec, spec, spec, P("head", None), P("head", None, None)),
            out_specs=spec,
            check_vma=False,
        )(queries, keys, values, vertical, slash)

    return run
```

```python
import functools
import math

import jax
import jax.numpy as jnp
from jax import lax
from jax.experimental import pallas as pl
from jax.experimental.pallas import tpu as pltpu
from jax.sharding import Mesh, PartitionSpec as P

BLK = 64
BIG = 1.0e30
LIVE, DEAD, OWN, PICKED = 0, 1, 2, 3
BF16, F32 = jnp.bfloat16, jnp.float32


def arrange_kernel(me_ref, k_ref, v_ref, *o_refs):
    mine, width, _ = o_refs[0].shape
    head_dim = o_refs[0].shape[2] - width
    for m, o_ref in enumerate(o_refs):
        device = lax.bitwise_xor(me_ref[0], m)
        first = way_of(device) * mine
        for h in range(mine):
            columns = pl.ds(pl.multiple_of((first + h) * head_dim, head_dim), head_dim)
            o_ref[h, :, :head_dim] = k_ref[:, columns]
            o_ref[h, :, head_dim:] = v_ref[:, columns].T


def arrange(me, keys, values, mine, head_dim):
    tok = keys.shape[0]
    vmem = pl.BlockSpec(memory_space=pltpu.VMEM)
    return pl.pallas_call(
        arrange_kernel,
        out_shape=[jax.ShapeDtypeStruct((mine, tok, head_dim + tok), BF16)] * 4,
        in_specs=[pl.BlockSpec(memory_space=pltpu.SMEM), vmem, vmem],
        out_specs=[vmem] * 4,
    )(me, keys, values)


def way_of(device):
    return lax.rem(device, 2) * 2 + lax.div(device, 2)


def collect_kernel(me_ref, own_ref, *rest):
    pieces, out_ref = rest[:3], rest[3]
    width = own_ref.shape[2]
    me = me_ref[0]
    for m in range(4):
        way = way_of(lax.bitwise_xor(me, m))
        columns = pl.ds(pl.multiple_of(way * width, width), width)
        out_ref[:, columns] = own_ref[way] if m == 0 else pieces[m - 1][...]


def collect(me, own, pieces):
    ways, tok, width = own.shape
    vmem = pl.BlockSpec(memory_space=pltpu.VMEM)
    return pl.pallas_call(
        collect_kernel,
        out_shape=jax.ShapeDtypeStruct((tok, ways * width), own.dtype),
        compiler_params=pltpu.CompilerParams(vmem_limit_bytes=8 << 20),
        in_specs=[pl.BlockSpec(memory_space=pltpu.SMEM)] + [vmem] * 4,
        out_specs=vmem,
    )(me, own, *pieces)


def step_kernel(code_ref, q_ref, pick_ref, *rest, parts, first, last, span, head_dim, group):
    part_refs = []
    for count in parts:
        part_refs.append(rest[:count])
        rest = rest[count:]
    if not first:
        (acc_in, stat_in, _), rest = rest[:3], rest[3:]
    if last:
        out_ref, rest = rest[0], rest[1:]
    else:
        (acc_out, stat_out, mark_out), rest = rest[:3], rest[3:]
        mark_out[...] = jnp.zeros(mark_out.shape, BF16)
    qext, etile, score_a, score_b = rest
    rows = BLK * group
    chunks, _, wide, _ = part_refs[0][0].shape
    per_part = chunks * wide // BLK
    slots = len(parts) * per_part
    size = per_part * BLK
    per_q = q_ref.shape[1] // BLK
    blocks_here = q_ref.shape[0] * per_q
    scale = math.log2(math.e) / math.sqrt(head_dim)

    token = lax.rem(lax.broadcasted_iota(jnp.int32, (rows, head_dim), 0), BLK)
    column = lax.broadcasted_iota(jnp.int32, (rows, head_dim), 1)
    masked = ((column < BLK) & (column > token)) | (column == BLK)
    qext[...] = jnp.where(masked, -BIG, 0.0).astype(BF16)
    key_iota = lax.broadcasted_iota(jnp.int32, (BLK, head_dim), 0)
    lane = lax.broadcasted_iota(jnp.int32, (BLK, head_dim), 1)
    etile[LIVE] = jnp.zeros((BLK, head_dim), BF16)
    etile[DEAD] = jnp.where(lane == BLK, 1.0, 0.0).astype(BF16)
    etile[OWN] = jnp.where(lane == key_iota, 1.0, 0.0).astype(BF16)

    def held(p, head, c):
        for ref in part_refs[p]:
            if head < ref.shape[1]:
                return ref.at[c, head]
            head -= ref.shape[1]

    def place(here, g):
        start = pl.multiple_of(lax.rem(here, per_q) * BLK, BLK)
        return lax.div(here, per_q), pl.ds(start, BLK), pl.ds(g * head_dim, head_dim)

    def stage(head, ahead, ahead_buffer, here, buffer, top):
        query = jnp.concatenate(
            [q_ref[place(ahead, head * group + g)] for g in range(group)], axis=0
        )
        query = jnp.concatenate([query, qext[...]], axis=1)
        at = head * blocks_here + here if here is not None else None
        if here is not None and not first:
            before = stat_in[at, :8]
            top = jnp.maximum(top, before)
            fade = jnp.exp2((before - top) * scale)
        ahead_top = jnp.full((8, rows), -jnp.inf, F32)
        shares, values = [], []
        for p in range(len(parts)):
            left = [held(p, head, c)[:, pl.ds(0, head_dim)] for c in range(chunks)]
            right = [
                etile[code_ref[head, ahead, p * per_part + i]] for i in range(per_part)
            ]
            key = jnp.concatenate(
                [jnp.concatenate(left, axis=0), jnp.concatenate(right, axis=0)], axis=1
            )
            tile = lax.dot_general(
                key, query, (((1,), (1,)), ((), ())), preferred_element_type=F32
            )
            ahead_buffer[pl.ds(p * size, size), :] = tile
            ahead_top = jnp.maximum(
                ahead_top, jnp.max(tile.reshape(size // 8, 8, rows), axis=0)
            )
            if here is not None:
                tile = buffer[pl.ds(p * size, size), :].reshape(size // 8, 8, rows)
                expo = jnp.exp2((tile - top[None]) * scale)
                shares.append(expo.reshape(size, rows).astype(BF16))
                values += [held(p, head, c)[:, pl.ds(head_dim, wide)] for c in range(chunks)]
        ahead_top = jnp.broadcast_to(jnp.max(ahead_top, axis=0, keepdims=True), (8, rows))
        if here is None:
            return ahead_top
        value = jnp.concatenate(values, axis=1)
        value = jnp.concatenate([value, jnp.ones((16, value.shape[1]), BF16)], axis=0)
        both = jnp.dot(value, jnp.concatenate(shares, axis=0), preferred_element_type=F32)
        mixed, weight = both[:head_dim], both[head_dim : head_dim + 8]
        if not first:
            mixed = mixed + acc_in[at] * fade[:1]
            weight = weight + stat_in[at, 8:] * fade
        if not last:
            acc_out[at] = mixed
            stat_out[at, :8] = top
            stat_out[at, 8:] = weight
            return ahead_top
        result = (mixed / weight[:1]).T.astype(BF16)
        for g in range(group):
            out_ref[place(here, (head - span[0]) * group + g)] = result[g * BLK : (g + 1) * BLK]
        return ahead_top

    for head in range(*span):
        for slot in range(slots):
            etile[PICKED + slot] = pick_ref[head, slot]

        def two(step, top):
            top = stage(head, 2 * step + 1, score_b, 2 * step, score_a, top)
            ahead = jnp.minimum(2 * step + 2, blocks_here - 1)
            return stage(head, ahead, score_a, 2 * step + 1, score_b, top)

        top = stage(head, 0, score_a, None, None, None)
        lax.fori_loop(0, blocks_here // 2, two, top)


def attend_step(code, query, pick, parts, state, span, last, head_dim, group):
    heads, slots = pick.shape[:2]
    blocks_here = query.shape[0] * query.shape[1] // BLK
    rows = BLK * group
    smem = pl.BlockSpec(memory_space=pltpu.SMEM)
    vmem = pl.BlockSpec(memory_space=pltpu.VMEM)
    carried = (
        jax.ShapeDtypeStruct((heads * blocks_here, head_dim, rows), F32),
        jax.ShapeDtypeStruct((heads * blocks_here, 16, rows), F32),
        jax.ShapeDtypeStruct((16, 128), BF16),
    )
    count = span[1] - span[0]
    out = jax.ShapeDtypeStruct(query.shape[:2] + (count * group * head_dim,), BF16)
    arrays = [x for part in parts for x in part]
    first = state is None
    state = () if first else tuple(state)
    work = count * blocks_here * rows * slots * BLK
    return pl.pallas_call(
        functools.partial(
            step_kernel,
            parts=tuple(len(part) for part in parts),
            first=first,
            last=last,
            span=span,
            head_dim=head_dim,
            group=group,
        ),
        out_shape=out if last else carried,
        in_specs=[smem] + [vmem] * (2 + len(arrays) + len(state)),
        out_specs=vmem if last else (vmem,) * 3,
        scratch_shapes=[
            pltpu.VMEM((rows, head_dim), BF16),
            pltpu.VMEM((PICKED + slots, BLK, head_dim), BF16),
            pltpu.VMEM((slots * BLK, rows), F32),
            pltpu.VMEM((slots * BLK, rows), F32),
        ],
        compiler_params=pltpu.CompilerParams(vmem_limit_bytes=16 << 20),
        cost_estimate=pl.CostEstimate(
            flops=4 * work * head_dim, transcendentals=work, bytes_accessed=8 << 20
        ),
    )(code, query, pick, *arrays, *state)


def body(queries, keys, values, vertical, slash, *, cores, chips, heads):
    tok, q_width = queries.shape
    all_heads = vertical.shape[0] * heads
    head_dim = keys.shape[1] // all_heads
    group = q_width // keys.shape[1]
    ways = cores * heads
    mine = all_heads // ways
    axes = ("head", "core") if cores > 1 else ("head",)
    groups = chips if cores > 1 else chips * 2
    per_group = tok * ways // BLK
    chip = lax.axis_index("chip")
    if cores == 1:
        chip = chip * 2 + lax.axis_index("core")
    relative = cores > 1 and chips == 8 and heads == 2
    swap = functools.partial(
        lax.all_to_all, axis_name=axes, split_axis=0, concat_axis=0, tiled=True
    )

    if relative:
        me = lax.axis_index("core") * 2 + lax.axis_index("head")
        me = me.astype(jnp.int32)
        pieces = arrange(me[None], keys, values, mine, head_dim)
        pair = [pieces[0]] + [
            lax.ppermute(pieces[m], ("core", "head"), [(i, i ^ m) for i in range(4)])
            for m in (1, 3, 2)
        ]
        pair = jnp.stack([pair[0], pair[1], pair[3], pair[2]])
    else:
        pair = jnp.concatenate(
            [keys.reshape(tok, ways, mine, head_dim), values.reshape(tok, ways, mine, head_dim)],
            axis=3,
        )
        pair = swap(pair.transpose(1, 2, 0, 3))
    query = queries.reshape(tok, ways, q_width // ways).transpose(1, 0, 2)

    pair, vertical, slash = lax.optimization_barrier((pair, vertical, slash))

    along = tok // BLK
    local = jnp.arange(per_group, dtype=jnp.int32)
    if cores > 1:
        local = local.reshape(cores, heads, along).swapaxes(0, 1).reshape(-1)
    local_keys = local
    if relative:
        order = jnp.stack([me ^ m for m in range(4)]).astype(jnp.int32)
        local_keys = (order[:, None] * along + jnp.arange(along, dtype=jnp.int32)).reshape(-1)
    first_head = lax.axis_index("core") * mine if cores > 1 else 0
    slash = lax.dynamic_slice_in_dim(slash, first_head, mine, axis=0)
    vertical = lax.dynamic_slice_in_dim(vertical, first_head, mine, axis=0)
    lists = lax.dynamic_slice_in_dim(slash, chip * per_group, per_group, axis=1)
    if cores > 1:
        lists = (
            lists.reshape(mine, cores, heads, along, -1).swapaxes(1, 2).reshape(lists.shape)
        )
    ids = chip * per_group + local

    def masks(source):
        nat = (source[:, None] * per_group + local_keys).reshape(-1)
        listed = jnp.any(lists[:, :, :, None] == nat, axis=2)
        slot = PICKED + jnp.arange(nat.shape[0], dtype=jnp.int32)
        code = jnp.where(
            listed,
            LIVE,
            jnp.where(nat == ids[:, None], OWN, jnp.where(nat > ids[:, None], DEAD, slot)),
        )
        position = nat[:, None] * BLK + jnp.arange(BLK, dtype=jnp.int32)
        hidden = jnp.all(vertical[:, None, None, :] != position[..., None], axis=3)
        lane = jnp.arange(head_dim, dtype=jnp.int32) == BLK
        return code, (hidden[..., None] & lane).astype(BF16)

    def attend(query, table, parts, state, last):
        state = None if state is None else tuple(state)
        run = functools.partial(attend_step, table[0], query, table[1], parts, state)
        if not last:
            return run((0, mine), False, head_dim, group)
        return run((0, mine), True, head_dim, group)

    state = None
    if relative:
        across = [(i, i ^ 1) for i in range(chips)]
        up = [(i, i + 2) for i in range(chips - 2)]
        final = chips // 2 - 1
        col = jnp.stack([chip % 2, 1 - chip % 2])
        tables = []
        for n in range(final + 1):
            row = chip // 2 - n
            tables.append(masks(jnp.where(row < 0, groups, 2 * row + col)))
        code, query = lax.optimization_barrier((tables[0][0], query))
        tables[0] = (code, tables[0][1])
        query = swap(query).reshape(-1, max(tok, BLK), q_width // ways)
        outward = [((me ^ m) & 1) * 2 + ((me ^ m) >> 1) for m in (1, 3, 2)]
        part, waiting = pair, None
        for n in range(final + 2):
            fetched = None
            if n <= final:
                if n == 1:
                    part, tables, outward = lax.optimization_barrier((part, tables, outward))
                if state is not None:
                    part, mark = lax.optimization_barrier((part, state[2]))
                    state = state[:2] + (mark,)
                if n < final or mine == 1:
                    other = (lax.ppermute(part, "chip", across),)
                else:
                    cut = (mine + 1) // 2
                    other = (
                        lax.ppermute(part[:, :cut], "chip", across),
                        lax.ppermute(waiting[1][0][:, cut:], "chip", up),
                    )
                fetched = ((part,), other)
                part = lax.ppermute(part, "chip", up) if n < final else None
            if n:
                state = attend(query, tables[n - 1], waiting, state, n > final)
            waiting = fetched
    else:
        query = swap(query).reshape(-1, max(tok, BLK), q_width // ways)
        axis = "chip" if cores > 1 else ("chip", "core")
        rows = pair.transpose(1, 0, 2, 3).reshape(mine, -1, 2 * head_dim)
        rows = lax.all_gather(rows, axis, axis=1, tiled=True)
        pieces = rows.shape[1] // (2 * BLK)
        turned = rows[..., head_dim:].reshape(mine, pieces, 2 * BLK, head_dim).swapaxes(2, 3)
        rows = rows[..., :head_dim].reshape(mine, pieces, 2 * BLK, head_dim)
        rows = jnp.concatenate([rows, turned], axis=3).swapaxes(0, 1)
        each = per_group // 2
        order = (chip + jnp.arange(groups, dtype=jnp.int32)) % groups
        rows = jnp.roll(rows.reshape((groups, each) + rows.shape[1:]), -chip, axis=0)
        many = math.gcd(groups, 4)
        for g in range(0, groups, many):
            part = rows[g : g + many].reshape((many * each,) + rows.shape[2:])
            state = attend(query, masks(order[g : g + many]), ((part,),), state, g + many == groups)

    if relative:
        pieces = {}
        zero = jnp.zeros((), jnp.int32)
        for m, way in zip((1, 3, 2), outward):
            piece = lax.dynamic_slice(
                state, (way, zero, zero), (1,) + state.shape[1:], allow_negative_indices=False
            )[0]
            pieces[m] = lax.ppermute(piece, ("core", "head"), [(i, i ^ m) for i in range(4)])
        return collect(me[None], state, [pieces[m] for m in (1, 2, 3)])
    out = swap(state.reshape(ways, tok, q_width // ways))
    return out.transpose(1, 0, 2).reshape(tok, q_width)


def solution(mesh):
    seq, heads = mesh.shape["seq"], mesh.shape["head"]
    split = Mesh(mesh.devices.reshape(seq // 2, 2, heads), ("chip", "core", "head"))
    spec = P(("chip", "core", "head"), None)

    def run(queries, keys, values, vertical, slash):
        local_heads = vertical.shape[0] // heads
        tok = queries.shape[0] // (seq * heads)
        cores = 2 if local_heads % 2 == 0 and tok % BLK == 0 else 1
        return jax.shard_map(
            functools.partial(body, cores=cores, chips=seq // 2, heads=heads),
            mesh=split,
            in_specs=(spec, spec, spec, P("head", None), P("head", None, None)),
            out_specs=spec,
            check_vma=False,
        )(queries, keys, values, vertical, slash)

    return run
```

```python
import functools
import math

import jax
import jax.numpy as jnp
from jax import lax
from jax.experimental import pallas as pl
from jax.experimental.pallas import tpu as pltpu
from jax.sharding import Mesh, PartitionSpec as P

BLK = 64
BIG = 1.0e30
LIVE, DEAD, OWN, PICKED = 0, 1, 2, 3
BF16, F32 = jnp.bfloat16, jnp.float32


def arrange_kernel(me_ref, k_ref, v_ref, *o_refs):
    mine, width, _ = o_refs[0].shape
    head_dim = o_refs[0].shape[2] - width
    for m, o_ref in enumerate(o_refs):
        device = lax.bitwise_xor(me_ref[0], m)
        first = way_of(device) * mine
        for h in range(mine):
            columns = pl.ds(pl.multiple_of((first + h) * head_dim, head_dim), head_dim)
            o_ref[h, :, :head_dim] = k_ref[:, columns]
            o_ref[h, :, head_dim:] = v_ref[:, columns].T


def arrange(me, keys, values, mine, head_dim):
    tok = keys.shape[0]
    vmem = pl.BlockSpec(memory_space=pltpu.VMEM)
    return pl.pallas_call(
        arrange_kernel,
        out_shape=[jax.ShapeDtypeStruct((mine, tok, head_dim + tok), BF16)] * 4,
        in_specs=[pl.BlockSpec(memory_space=pltpu.SMEM), vmem, vmem],
        out_specs=[vmem] * 4,
    )(me, keys, values)


def way_of(device):
    return lax.rem(device, 2) * 2 + lax.div(device, 2)


def collect_kernel(me_ref, own_ref, *rest):
    pieces, out_ref = rest[:3], rest[3]
    width = own_ref.shape[2]
    me = me_ref[0]
    for m in range(4):
        way = way_of(lax.bitwise_xor(me, m))
        columns = pl.ds(pl.multiple_of(way * width, width), width)
        out_ref[:, columns] = own_ref[0] if m == 0 else pieces[m - 1][...]


def collect(me, own, pieces):
    ways, tok, width = own.shape
    vmem = pl.BlockSpec(memory_space=pltpu.VMEM)
    return pl.pallas_call(
        collect_kernel,
        out_shape=jax.ShapeDtypeStruct((tok, ways * width), own.dtype),
        compiler_params=pltpu.CompilerParams(vmem_limit_bytes=8 << 20),
        in_specs=[pl.BlockSpec(memory_space=pltpu.SMEM)] + [vmem] * 4,
        out_specs=vmem,
    )(me, own, *pieces)


def step_kernel(code_ref, q_ref, pick_ref, *rest, parts, first, last, span, head_dim, group):
    part_refs = []
    for count in parts:
        part_refs.append(rest[:count])
        rest = rest[count:]
    if not first:
        (acc_in, stat_in, _), rest = rest[:3], rest[3:]
    if last:
        out_ref, rest = rest[0], rest[1:]
    else:
        (acc_out, stat_out, mark_out), rest = rest[:3], rest[3:]
        mark_out[...] = jnp.zeros(mark_out.shape, BF16)
    qext, etile, score_a, score_b = rest
    rows = BLK * group
    chunks, _, wide, _ = part_refs[0][0].shape
    per_part = chunks * wide // BLK
    slots = len(parts) * per_part
    size = per_part * BLK
    per_q = q_ref.shape[1] // BLK
    blocks_here = q_ref.shape[0] * per_q
    scale = math.log2(math.e) / math.sqrt(head_dim)

    token = lax.rem(lax.broadcasted_iota(jnp.int32, (rows, head_dim), 0), BLK)
    column = lax.broadcasted_iota(jnp.int32, (rows, head_dim), 1)
    masked = ((column < BLK) & (column > token)) | (column == BLK)
    qext[...] = jnp.where(masked, -BIG, 0.0).astype(BF16)
    key_iota = lax.broadcasted_iota(jnp.int32, (BLK, head_dim), 0)
    lane = lax.broadcasted_iota(jnp.int32, (BLK, head_dim), 1)
    etile[LIVE] = jnp.zeros((BLK, head_dim), BF16)
    etile[DEAD] = jnp.where(lane == BLK, 1.0, 0.0).astype(BF16)
    etile[OWN] = jnp.where(lane == key_iota, 1.0, 0.0).astype(BF16)

    def held(p, head, c):
        for ref in part_refs[p]:
            if head < ref.shape[1]:
                return ref.at[c, head]
            head -= ref.shape[1]

    def place(here, g):
        start = pl.multiple_of(lax.rem(here, per_q) * BLK, BLK)
        return lax.div(here, per_q), pl.ds(start, BLK), pl.ds(g * head_dim, head_dim)

    def stage(head, ahead, ahead_buffer, here, buffer, top):
        query = jnp.concatenate(
            [q_ref[place(ahead, head * group + g)] for g in range(group)], axis=0
        )
        query = jnp.concatenate([query, qext[...]], axis=1)
        at = head * blocks_here + here if here is not None else None
        if here is not None and not first:
            before = stat_in[at, :8]
            top = jnp.maximum(top, before)
            fade = jnp.exp2((before - top) * scale)
        ahead_top = jnp.full((8, rows), -jnp.inf, F32)
        shares, values = [], []
        for p in range(len(parts)):
            left = [held(p, head, c)[:, pl.ds(0, head_dim)] for c in range(chunks)]
            right = [
                etile[code_ref[head, ahead, p * per_part + i]] for i in range(per_part)
            ]
            key = jnp.concatenate(
                [jnp.concatenate(left, axis=0), jnp.concatenate(right, axis=0)], axis=1
            )
            tile = lax.dot_general(
                key, query, (((1,), (1,)), ((), ())), preferred_element_type=F32
            )
            ahead_buffer[pl.ds(p * size, size), :] = tile
            ahead_top = jnp.maximum(
                ahead_top, jnp.max(tile.reshape(size // 8, 8, rows), axis=0)
            )
            if here is not None:
                tile = buffer[pl.ds(p * size, size), :].reshape(size // 8, 8, rows)
                expo = jnp.exp2((tile - top[None]) * scale)
                shares.append(expo.reshape(size, rows).astype(BF16))
                values += [held(p, head, c)[:, pl.ds(head_dim, wide)] for c in range(chunks)]
        ahead_top = jnp.broadcast_to(jnp.max(ahead_top, axis=0, keepdims=True), (8, rows))
        if here is None:
            return ahead_top
        value = jnp.concatenate(values, axis=1)
        value = jnp.concatenate([value, jnp.ones((16, value.shape[1]), BF16)], axis=0)
        both = jnp.dot(value, jnp.concatenate(shares, axis=0), preferred_element_type=F32)
        mixed, weight = both[:head_dim], both[head_dim : head_dim + 8]
        if not first:
            mixed = mixed + acc_in[at] * fade[:1]
            weight = weight + stat_in[at, 8:] * fade
        if not last:
            acc_out[at] = mixed
            stat_out[at, :8] = top
            stat_out[at, 8:] = weight
            return ahead_top
        result = (mixed / weight[:1]).T.astype(BF16)
        for g in range(group):
            out_ref[place(here, (head - span[0]) * group + g)] = result[g * BLK : (g + 1) * BLK]
        return ahead_top

    for head in range(*span):
        for slot in range(slots):
            etile[PICKED + slot] = pick_ref[head, slot]

        def two(step, top):
            top = stage(head, 2 * step + 1, score_b, 2 * step, score_a, top)
            ahead = jnp.minimum(2 * step + 2, blocks_here - 1)
            return stage(head, ahead, score_a, 2 * step + 1, score_b, top)

        top = stage(head, 0, score_a, None, None, None)
        lax.fori_loop(0, blocks_here // 2, two, top)


def attend_step(code, query, pick, parts, state, span, last, head_dim, group):
    heads, slots = pick.shape[:2]
    blocks_here = query.shape[0] * query.shape[1] // BLK
    rows = BLK * group
    smem = pl.BlockSpec(memory_space=pltpu.SMEM)
    vmem = pl.BlockSpec(memory_space=pltpu.VMEM)
    carried = (
        jax.ShapeDtypeStruct((heads * blocks_here, head_dim, rows), F32),
        jax.ShapeDtypeStruct((heads * blocks_here, 16, rows), F32),
        jax.ShapeDtypeStruct((16, 128), BF16),
    )
    count = span[1] - span[0]
    out = jax.ShapeDtypeStruct(query.shape[:2] + (count * group * head_dim,), BF16)
    arrays = [x for part in parts for x in part]
    first = state is None
    state = () if first else tuple(state)
    work = count * blocks_here * rows * slots * BLK
    return pl.pallas_call(
        functools.partial(
            step_kernel,
            parts=tuple(len(part) for part in parts),
            first=first,
            last=last,
            span=span,
            head_dim=head_dim,
            group=group,
        ),
        out_shape=out if last else carried,
        in_specs=[smem] + [vmem] * (2 + len(arrays) + len(state)),
        out_specs=vmem if last else (vmem,) * 3,
        scratch_shapes=[
            pltpu.VMEM((rows, head_dim), BF16),
            pltpu.VMEM((PICKED + slots, BLK, head_dim), BF16),
            pltpu.VMEM((slots * BLK, rows), F32),
            pltpu.VMEM((slots * BLK, rows), F32),
        ],
        compiler_params=pltpu.CompilerParams(vmem_limit_bytes=16 << 20),
        cost_estimate=pl.CostEstimate(
            flops=4 * work * head_dim, transcendentals=work, bytes_accessed=8 << 20
        ),
    )(code, query, pick, *arrays, *state)


def body(queries, keys, values, vertical, slash, *, cores, chips, heads):
    tok, q_width = queries.shape
    all_heads = vertical.shape[0] * heads
    head_dim = keys.shape[1] // all_heads
    group = q_width // keys.shape[1]
    ways = cores * heads
    mine = all_heads // ways
    axes = ("head", "core") if cores > 1 else ("head",)
    groups = chips if cores > 1 else chips * 2
    per_group = tok * ways // BLK
    chip = lax.axis_index("chip")
    if cores == 1:
        chip = chip * 2 + lax.axis_index("core")
    relative = cores > 1 and chips == 8 and heads == 2
    swap = functools.partial(
        lax.all_to_all, axis_name=axes, split_axis=0, concat_axis=0, tiled=True
    )

    if relative:
        me = lax.axis_index("core") * 2 + lax.axis_index("head")
        me = me.astype(jnp.int32)
        pieces = arrange(me[None], keys, values, mine, head_dim)
        pair = [pieces[0]] + [
            lax.ppermute(pieces[m], ("core", "head"), [(i, i ^ m) for i in range(4)])
            for m in (1, 3, 2)
        ]
        pair = jnp.stack([pair[0], pair[1], pair[3], pair[2]])
    else:
        pair = jnp.concatenate(
            [keys.reshape(tok, ways, mine, head_dim), values.reshape(tok, ways, mine, head_dim)],
            axis=3,
        )
        pair = swap(pair.transpose(1, 2, 0, 3))
    zero = jnp.zeros((), jnp.int32)
    if relative:
        wide = q_width // ways
        outward = [((me ^ m) & 1) * 2 + ((me ^ m) >> 1) for m in range(4)]
        query = [
            lax.dynamic_slice(
                queries, (zero, way * wide), (tok, wide), allow_negative_indices=False
            )
            for way in outward
        ]
    else:
        query = queries.reshape(tok, ways, q_width // ways).transpose(1, 0, 2)

    pair, vertical, slash = lax.optimization_barrier((pair, vertical, slash))

    along = tok // BLK
    local = jnp.arange(per_group, dtype=jnp.int32)
    if cores > 1:
        local = local.reshape(cores, heads, along).swapaxes(0, 1).reshape(-1)
    local_keys = local
    if relative:
        order = jnp.stack([me ^ m for m in range(4)]).astype(jnp.int32)
        local_keys = (order[:, None] * along + jnp.arange(along, dtype=jnp.int32)).reshape(-1)
    first_head = lax.axis_index("core") * mine if cores > 1 else 0
    slash = lax.dynamic_slice_in_dim(slash, first_head, mine, axis=0)
    vertical = lax.dynamic_slice_in_dim(vertical, first_head, mine, axis=0)
    lists = lax.dynamic_slice_in_dim(slash, chip * per_group, per_group, axis=1)
    if relative:
        four = lists.reshape(mine, 2, 2, along, -1)
        four = jnp.where(me >> 1 == 1, four[:, ::-1], four)
        four = jnp.where(me & 1 == 1, four[:, :, ::-1], four)
        lists = four.reshape(lists.shape)
    elif cores > 1:
        lists = (
            lists.reshape(mine, cores, heads, along, -1).swapaxes(1, 2).reshape(lists.shape)
        )
    ids = chip * per_group + (local_keys if relative else local)

    def masks(source):
        nat = (source[:, None] * per_group + local_keys).reshape(-1)
        listed = jnp.any(lists[:, :, :, None] == nat, axis=2)
        slot = PICKED + jnp.arange(nat.shape[0], dtype=jnp.int32)
        code = jnp.where(
            listed,
            LIVE,
            jnp.where(nat == ids[:, None], OWN, jnp.where(nat > ids[:, None], DEAD, slot)),
        )
        position = nat[:, None] * BLK + jnp.arange(BLK, dtype=jnp.int32)
        hidden = jnp.all(vertical[:, None, None, :] != position[..., None], axis=3)
        lane = jnp.arange(head_dim, dtype=jnp.int32) == BLK
        return code, (hidden[..., None] & lane).astype(BF16)

    def attend(query, table, parts, state, last):
        state = None if state is None else tuple(state)
        run = functools.partial(attend_step, table[0], query, table[1], parts, state)
        if not last:
            return run((0, mine), False, head_dim, group)
        return run((0, mine), True, head_dim, group)

    state = None
    if relative:
        across = [(i, i ^ 1) for i in range(chips)]
        up = [(i, i + 2) for i in range(chips - 2)]
        final = chips // 2 - 1
        col = jnp.stack([chip % 2, 1 - chip % 2])
        tables = []
        for n in range(final + 1):
            row = chip // 2 - n
            tables.append(masks(jnp.where(row < 0, groups, 2 * row + col)))
        code, query = lax.optimization_barrier((tables[0][0], query))
        tables[0] = (code, tables[0][1])
        query = {0: query[0]} | {
            m: lax.ppermute(query[m], ("core", "head"), [(i, i ^ m) for i in range(4)])
            for m in (1, 3, 2)
        }
        query = jnp.stack([query[m] for m in range(4)])
        part, waiting = pair, None
        for n in range(final + 2):
            fetched = None
            if n <= final:
                if n == 1:
                    part, tables = lax.optimization_barrier((part, tables))
                if state is not None:
                    part, mark = lax.optimization_barrier((part, state[2]))
                    state = state[:2] + (mark,)
                if n < final or mine == 1:
                    other = (lax.ppermute(part, "chip", across),)
                else:
                    cut = (mine + 1) // 2
                    other = (
                        lax.ppermute(part[:, :cut], "chip", across),
                        lax.ppermute(waiting[1][0][:, cut:], "chip", up),
                    )
                fetched = ((part,), other)
                part = lax.ppermute(part, "chip", up) if n < final else None
            if n:
                state = attend(query, tables[n - 1], waiting, state, n > final)
            waiting = fetched
    else:
        query = swap(query).reshape(-1, max(tok, BLK), q_width // ways)
        axis = "chip" if cores > 1 else ("chip", "core")
        rows = pair.transpose(1, 0, 2, 3).reshape(mine, -1, 2 * head_dim)
        rows = lax.all_gather(rows, axis, axis=1, tiled=True)
        pieces = rows.shape[1] // (2 * BLK)
        turned = rows[..., head_dim:].reshape(mine, pieces, 2 * BLK, head_dim).swapaxes(2, 3)
        rows = rows[..., :head_dim].reshape(mine, pieces, 2 * BLK, head_dim)
        rows = jnp.concatenate([rows, turned], axis=3).swapaxes(0, 1)
        each = per_group // 2
        order = (chip + jnp.arange(groups, dtype=jnp.int32)) % groups
        rows = jnp.roll(rows.reshape((groups, each) + rows.shape[1:]), -chip, axis=0)
        many = math.gcd(groups, 4)
        for g in range(0, groups, many):
            part = rows[g : g + many].reshape((many * each,) + rows.shape[2:])
            state = attend(query, masks(order[g : g + many]), ((part,),), state, g + many == groups)

    if relative:
        pieces = {
            m: lax.ppermute(state[m], ("core", "head"), [(i, i ^ m) for i in range(4)])
            for m in (1, 3, 2)
        }
        return collect(me[None], state, [pieces[m] for m in (1, 2, 3)])
    out = swap(state.reshape(ways, tok, q_width // ways))
    return out.transpose(1, 0, 2).reshape(tok, q_width)


def solution(mesh):
    seq, heads = mesh.shape["seq"], mesh.shape["head"]
    split = Mesh(mesh.devices.reshape(seq // 2, 2, heads), ("chip", "core", "head"))
    spec = P(("chip", "core", "head"), None)

    def run(queries, keys, values, vertical, slash):
        local_heads = vertical.shape[0] // heads
        tok = queries.shape[0] // (seq * heads)
        cores = 2 if local_heads % 2 == 0 and tok % BLK == 0 else 1
        return jax.shard_map(
            functools.partial(body, cores=cores, chips=seq // 2, heads=heads),
            mesh=split,
            in_specs=(spec, spec, spec, P("head", None), P("head", None, None)),
            out_specs=spec,
            check_vma=False,
        )(queries, keys, values, vertical, slash)

    return run
```

```python
import functools
import math

import jax
import jax.numpy as jnp
from jax import lax
from jax.experimental import pallas as pl
from jax.experimental.pallas import tpu as pltpu
from jax.sharding import Mesh, PartitionSpec as P

BLK = 64
BIG = 1.0e30
LIVE, DEAD, OWN, PICKED = 0, 1, 2, 3
BF16, F32 = jnp.bfloat16, jnp.float32


def arrange_kernel(me_ref, k_ref, v_ref, *o_refs):
    mine, width, _ = o_refs[0].shape
    head_dim = o_refs[0].shape[2] - width
    for m, o_ref in enumerate(o_refs):
        device = lax.bitwise_xor(me_ref[0], m)
        first = way_of(device) * mine
        for h in range(mine):
            columns = pl.ds(pl.multiple_of((first + h) * head_dim, head_dim), head_dim)
            o_ref[h, :, :head_dim] = k_ref[:, columns]
            o_ref[h, :, head_dim:] = v_ref[:, columns].T


def arrange(me, keys, values, mine, head_dim):
    tok = keys.shape[0]
    vmem = pl.BlockSpec(memory_space=pltpu.VMEM)
    return pl.pallas_call(
        arrange_kernel,
        out_shape=[jax.ShapeDtypeStruct((mine, tok, head_dim + tok), BF16)] * 4,
        in_specs=[pl.BlockSpec(memory_space=pltpu.SMEM), vmem, vmem],
        out_specs=[vmem] * 4,
    )(me, keys, values)


def way_of(device):
    return lax.rem(device, 2) * 2 + lax.div(device, 2)


def collect_kernel(me_ref, own_ref, *rest):
    pieces, out_ref = rest[:3], rest[3]
    width = own_ref.shape[2]
    me = me_ref[0]
    for m in range(4):
        way = way_of(lax.bitwise_xor(me, m))
        columns = pl.ds(pl.multiple_of(way * width, width), width)
        out_ref[:, columns] = own_ref[0] if m == 0 else pieces[m - 1][...]


def collect(me, own, pieces):
    ways, tok, width = own.shape
    vmem = pl.BlockSpec(memory_space=pltpu.VMEM)
    return pl.pallas_call(
        collect_kernel,
        out_shape=jax.ShapeDtypeStruct((tok, ways * width), own.dtype),
        compiler_params=pltpu.CompilerParams(vmem_limit_bytes=8 << 20),
        in_specs=[pl.BlockSpec(memory_space=pltpu.SMEM)] + [vmem] * 4,
        out_specs=vmem,
    )(me, own, *pieces)


def step_kernel(code_ref, q_ref, pick_ref, *rest, parts, first, last, span, head_dim, group):
    part_refs = []
    for count in parts:
        part_refs.append(rest[:count])
        rest = rest[count:]
    if not first:
        (acc_in, stat_in, _), rest = rest[:3], rest[3:]
    if last:
        out_ref, rest = rest[0], rest[1:]
    else:
        (acc_out, stat_out, mark_out), rest = rest[:3], rest[3:]
        mark_out[...] = jnp.zeros(mark_out.shape, BF16)
    qext, etile, score_a, score_b = rest
    rows = BLK * group
    chunks, _, wide, _ = part_refs[0][0].shape
    per_part = chunks * wide // BLK
    slots = len(parts) * per_part
    size = per_part * BLK
    per_q = q_ref.shape[1] // BLK
    blocks_here = q_ref.shape[0] * per_q
    scale = math.log2(math.e) / math.sqrt(head_dim)

    token = lax.rem(lax.broadcasted_iota(jnp.int32, (rows, head_dim), 0), BLK)
    column = lax.broadcasted_iota(jnp.int32, (rows, head_dim), 1)
    masked = ((column < BLK) & (column > token)) | (column == BLK)
    qext[...] = jnp.where(masked, -BIG, 0.0).astype(BF16)
    key_iota = lax.broadcasted_iota(jnp.int32, (BLK, head_dim), 0)
    lane = lax.broadcasted_iota(jnp.int32, (BLK, head_dim), 1)
    each = PICKED + slots
    for head in range(*span):
        base = head * each
        etile[base + LIVE] = jnp.zeros((BLK, head_dim), BF16)
        etile[base + DEAD] = jnp.where(lane == BLK, 1.0, 0.0).astype(BF16)
        etile[base + OWN] = jnp.where(lane == key_iota, 1.0, 0.0).astype(BF16)
        for slot in range(slots):
            etile[base + PICKED + slot] = pick_ref[head, slot]

    def held(p, head, c):
        for ref in part_refs[p]:
            if head < ref.shape[1]:
                return ref.at[c, head]
            head -= ref.shape[1]

    def place(here, g):
        start = pl.multiple_of(lax.rem(here, per_q) * BLK, BLK)
        return lax.div(here, per_q), pl.ds(start, BLK), pl.ds(g * head_dim, head_dim)

    def stage(next_head, ahead, ahead_buffer, head, here, buffer, top):
        if ahead is not None:
            query = jnp.concatenate(
                [q_ref[place(ahead, next_head * group + g)] for g in range(group)], axis=0
            )
            query = jnp.concatenate([query, qext[...]], axis=1)
        at = head * blocks_here + here if here is not None else None
        if here is not None and not first:
            before = stat_in[at, :8]
            top = jnp.maximum(top, before)
            fade = jnp.exp2((before - top) * scale)
        ahead_top = jnp.full((8, rows), -jnp.inf, F32)
        shares, values = [], []
        for p in range(len(parts)):
            if ahead is not None:
                left = [held(p, next_head, c)[:, pl.ds(0, head_dim)] for c in range(chunks)]
                right = [
                    etile[next_head * each + code_ref[next_head, ahead, p * per_part + i]]
                    for i in range(per_part)
                ]
                key = jnp.concatenate(
                    [jnp.concatenate(left, axis=0), jnp.concatenate(right, axis=0)], axis=1
                )
                tile = lax.dot_general(
                    key, query, (((1,), (1,)), ((), ())), preferred_element_type=F32
                )
                ahead_buffer[pl.ds(p * size, size), :] = tile
                ahead_top = jnp.maximum(
                    ahead_top, jnp.max(tile.reshape(size // 8, 8, rows), axis=0)
                )
            if here is not None:
                tile = buffer[pl.ds(p * size, size), :].reshape(size // 8, 8, rows)
                expo = jnp.exp2((tile - top[None]) * scale)
                shares.append(expo.reshape(size, rows).astype(BF16))
                values += [held(p, head, c)[:, pl.ds(head_dim, wide)] for c in range(chunks)]
        ahead_top = jnp.broadcast_to(jnp.max(ahead_top, axis=0, keepdims=True), (8, rows))
        if here is None:
            return ahead_top
        value = jnp.concatenate(values, axis=1)
        value = jnp.concatenate([value, jnp.ones((16, value.shape[1]), BF16)], axis=0)
        both = jnp.dot(value, jnp.concatenate(shares, axis=0), preferred_element_type=F32)
        mixed, weight = both[:head_dim], both[head_dim : head_dim + 8]
        if not first:
            mixed = mixed + acc_in[at] * fade[:1]
            weight = weight + stat_in[at, 8:] * fade
        if not last:
            acc_out[at] = mixed
            stat_out[at, :8] = top
            stat_out[at, 8:] = weight
            return ahead_top
        result = (mixed / weight[:1]).T.astype(BF16)
        for g in range(group):
            out_ref[place(here, (head - span[0]) * group + g)] = result[g * BLK : (g + 1) * BLK]
        return ahead_top

    top = stage(span[0], 0, score_a, None, None, None, None)
    final = blocks_here - 1
    for head in range(*span):

        def two(step, top):
            top = stage(head, 2 * step + 1, score_b, head, 2 * step, score_a, top)
            return stage(head, 2 * step + 2, score_a, head, 2 * step + 1, score_b, top)

        top = lax.fori_loop(0, blocks_here // 2 - 1, two, top)
        top = stage(head, final, score_b, head, final - 1, score_a, top)
        following = 0 if head + 1 < span[1] else None
        top = stage(head + 1, following, score_a, head, final, score_b, top)


def attend_step(code, query, pick, parts, state, span, last, head_dim, group):
    heads, slots = pick.shape[:2]
    blocks_here = query.shape[0] * query.shape[1] // BLK
    rows = BLK * group
    smem = pl.BlockSpec(memory_space=pltpu.SMEM)
    vmem = pl.BlockSpec(memory_space=pltpu.VMEM)
    carried = (
        jax.ShapeDtypeStruct((heads * blocks_here, head_dim, rows), F32),
        jax.ShapeDtypeStruct((heads * blocks_here, 16, rows), F32),
        jax.ShapeDtypeStruct((16, 128), BF16),
    )
    count = span[1] - span[0]
    out = jax.ShapeDtypeStruct(query.shape[:2] + (count * group * head_dim,), BF16)
    arrays = [x for part in parts for x in part]
    first = state is None
    state = () if first else tuple(state)
    work = count * blocks_here * rows * slots * BLK
    return pl.pallas_call(
        functools.partial(
            step_kernel,
            parts=tuple(len(part) for part in parts),
            first=first,
            last=last,
            span=span,
            head_dim=head_dim,
            group=group,
        ),
        out_shape=out if last else carried,
        in_specs=[smem] + [vmem] * (2 + len(arrays) + len(state)),
        out_specs=vmem if last else (vmem,) * 3,
        scratch_shapes=[
            pltpu.VMEM((rows, head_dim), BF16),
            pltpu.VMEM((heads * (PICKED + slots), BLK, head_dim), BF16),
            pltpu.VMEM((slots * BLK, rows), F32),
            pltpu.VMEM((slots * BLK, rows), F32),
        ],
        compiler_params=pltpu.CompilerParams(vmem_limit_bytes=16 << 20),
        cost_estimate=pl.CostEstimate(
            flops=4 * work * head_dim, transcendentals=work, bytes_accessed=8 << 20
        ),
    )(code, query, pick, *arrays, *state)


def body(queries, keys, values, vertical, slash, *, cores, chips, heads):
    tok, q_width = queries.shape
    all_heads = vertical.shape[0] * heads
    head_dim = keys.shape[1] // all_heads
    group = q_width // keys.shape[1]
    ways = cores * heads
    mine = all_heads // ways
    axes = ("head", "core") if cores > 1 else ("head",)
    groups = chips if cores > 1 else chips * 2
    per_group = tok * ways // BLK
    chip = lax.axis_index("chip")
    if cores == 1:
        chip = chip * 2 + lax.axis_index("core")
    relative = cores > 1 and chips == 8 and heads == 2
    swap = functools.partial(
        lax.all_to_all, axis_name=axes, split_axis=0, concat_axis=0, tiled=True
    )

    if relative:
        me = lax.axis_index("core") * 2 + lax.axis_index("head")
        me = me.astype(jnp.int32)
        pieces = arrange(me[None], keys, values, mine, head_dim)
        pair = [pieces[0]] + [
            lax.ppermute(pieces[m], ("core", "head"), [(i, i ^ m) for i in range(4)])
            for m in (1, 3, 2)
        ]
        pair = jnp.stack([pair[0], pair[1], pair[3], pair[2]])
    else:
        pair = jnp.concatenate(
            [keys.reshape(tok, ways, mine, head_dim), values.reshape(tok, ways, mine, head_dim)],
            axis=3,
        )
        pair = swap(pair.transpose(1, 2, 0, 3))
    zero = jnp.zeros((), jnp.int32)
    if relative:
        wide = q_width // ways
        outward = [((me ^ m) & 1) * 2 + ((me ^ m) >> 1) for m in range(4)]
        query = [
            lax.dynamic_slice(
                queries, (zero, way * wide), (tok, wide), allow_negative_indices=False
            )
            for way in outward
        ]
    else:
        query = queries.reshape(tok, ways, q_width // ways).transpose(1, 0, 2)

    pair, vertical, slash = lax.optimization_barrier((pair, vertical, slash))

    along = tok // BLK
    local = jnp.arange(per_group, dtype=jnp.int32)
    if cores > 1:
        local = local.reshape(cores, heads, along).swapaxes(0, 1).reshape(-1)
    local_keys = local
    if relative:
        order = jnp.stack([me ^ m for m in range(4)]).astype(jnp.int32)
        local_keys = (order[:, None] * along + jnp.arange(along, dtype=jnp.int32)).reshape(-1)
    first_head = lax.axis_index("core") * mine if cores > 1 else 0
    slash = lax.dynamic_slice_in_dim(slash, first_head, mine, axis=0)
    vertical = lax.dynamic_slice_in_dim(vertical, first_head, mine, axis=0)
    lists = lax.dynamic_slice_in_dim(slash, chip * per_group, per_group, axis=1)
    if relative:
        four = lists.reshape(mine, 2, 2, along, -1)
        four = jnp.where(me >> 1 == 1, four[:, ::-1], four)
        four = jnp.where(me & 1 == 1, four[:, :, ::-1], four)
        lists = four.reshape(lists.shape)
    elif cores > 1:
        lists = (
            lists.reshape(mine, cores, heads, along, -1).swapaxes(1, 2).reshape(lists.shape)
        )
    ids = chip * per_group + (local_keys if relative else local)

    def masks(source):
        nat = (source[:, None] * per_group + local_keys).reshape(-1)
        listed = jnp.any(lists[:, :, :, None] == nat, axis=2)
        slot = PICKED + jnp.arange(nat.shape[0], dtype=jnp.int32)
        code = jnp.where(
            listed,
            LIVE,
            jnp.where(nat == ids[:, None], OWN, jnp.where(nat > ids[:, None], DEAD, slot)),
        )
        position = nat[:, None] * BLK + jnp.arange(BLK, dtype=jnp.int32)
        hidden = jnp.all(vertical[:, None, None, :] != position[..., None], axis=3)
        lane = jnp.arange(head_dim, dtype=jnp.int32) == BLK
        return code, (hidden[..., None] & lane).astype(BF16)

    def attend(query, table, parts, state, last):
        state = None if state is None else tuple(state)
        run = functools.partial(attend_step, table[0], query, table[1], parts, state)
        if not last:
            return run((0, mine), False, head_dim, group)
        return run((0, mine), True, head_dim, group)

    state = None
    if relative:
        across = [(i, i ^ 1) for i in range(chips)]
        up = [(i, i + 2) for i in range(chips - 2)]
        final = chips // 2 - 1
        col = jnp.stack([chip % 2, 1 - chip % 2])
        tables = []
        for n in range(final + 1):
            row = chip // 2 - n
            tables.append(masks(jnp.where(row < 0, groups, 2 * row + col)))
        code, query = lax.optimization_barrier((tables[0][0], query))
        tables[0] = (code, tables[0][1])
        query = {0: query[0]} | {
            m: lax.ppermute(query[m], ("core", "head"), [(i, i ^ m) for i in range(4)])
            for m in (1, 3, 2)
        }
        query = jnp.stack([query[m] for m in range(4)])
        part, waiting = pair, None
        for n in range(final + 2):
            fetched = None
            if n <= final:
                if n == 1:
                    part, tables = lax.optimization_barrier((part, tables))
                if state is not None:
                    part, mark = lax.optimization_barrier((part, state[2]))
                    state = state[:2] + (mark,)
                if n < final or mine == 1:
                    other = (lax.ppermute(part, "chip", across),)
                else:
                    cut = (mine + 1) // 2
                    other = (
                        lax.ppermute(part[:, :cut], "chip", across),
                        lax.ppermute(waiting[1][0][:, cut:], "chip", up),
                    )
                fetched = ((part,), other)
                part = lax.ppermute(part, "chip", up) if n < final else None
            if n:
                state = attend(query, tables[n - 1], waiting, state, n > final)
            waiting = fetched
    else:
        query = swap(query).reshape(-1, max(tok, BLK), q_width // ways)
        axis = "chip" if cores > 1 else ("chip", "core")
        rows = pair.transpose(1, 0, 2, 3).reshape(mine, -1, 2 * head_dim)
        rows = lax.all_gather(rows, axis, axis=1, tiled=True)
        pieces = rows.shape[1] // (2 * BLK)
        turned = rows[..., head_dim:].reshape(mine, pieces, 2 * BLK, head_dim).swapaxes(2, 3)
        rows = rows[..., :head_dim].reshape(mine, pieces, 2 * BLK, head_dim)
        rows = jnp.concatenate([rows, turned], axis=3).swapaxes(0, 1)
        each = per_group // 2
        order = (chip + jnp.arange(groups, dtype=jnp.int32)) % groups
        rows = jnp.roll(rows.reshape((groups, each) + rows.shape[1:]), -chip, axis=0)
        many = math.gcd(groups, 4)
        for g in range(0, groups, many):
            part = rows[g : g + many].reshape((many * each,) + rows.shape[2:])
            state = attend(query, masks(order[g : g + many]), ((part,),), state, g + many == groups)

    if relative:
        pieces = {
            m: lax.ppermute(state[m], ("core", "head"), [(i, i ^ m) for i in range(4)])
            for m in (1, 3, 2)
        }
        return collect(me[None], state, [pieces[m] for m in (1, 2, 3)])
    out = swap(state.reshape(ways, tok, q_width // ways))
    return out.transpose(1, 0, 2).reshape(tok, q_width)


def solution(mesh):
    seq, heads = mesh.shape["seq"], mesh.shape["head"]
    split = Mesh(mesh.devices.reshape(seq // 2, 2, heads), ("chip", "core", "head"))
    spec = P(("chip", "core", "head"), None)

    def run(queries, keys, values, vertical, slash):
        local_heads = vertical.shape[0] // heads
        tok = queries.shape[0] // (seq * heads)
        cores = 2 if local_heads % 2 == 0 and tok % BLK == 0 else 1
        return jax.shard_map(
            functools.partial(body, cores=cores, chips=seq // 2, heads=heads),
            mesh=split,
            in_specs=(spec, spec, spec, P("head", None), P("head", None, None)),
            out_specs=spec,
            check_vma=False,
        )(queries, keys, values, vertical, slash)

    return run
```
